128 devices in a mesh: dp: 16 (over x, y), cent: 8 (over z, core).
Axes of the slice: x: 4, y: 4, z: 4, core: 2. Of those that a mesh axis runs over, the one named last changes fastest.
Arguments:
- embeddings: bfloat16 [65536, 1024], P('dp'), may hold values from -2000 to 2000
- centroids: bfloat16 [16384, 1024], P('cent'), may hold values from -2000 to 2000
- kmeans_id: int32 [65536], P('dp'), may hold values from 0 to 16383, as said below
- members: int32 [512, 16, 16], P(None, 'dp'), may hold values from 0 to 4095, as said below
- counts: int32 [512, 16], P(None, 'dp'), may hold values from 4 to 16, as said below
- owner_groups: int32 [16, 8, 4], replicated, may hold values from 0 to 511, as said below
Outputs:
- best_score: float32 [65536], P('dp')
- new_centroids: float32 [1024, 16384], P('dp', 'cent')
- slot_max: float32 [16, 8, 4, 256], P('dp', 'cent')
The draws below stay inside these ranges and needn't reach their ends.
Inputs may be any that keep to these rules, and one draw needn't show every extreme that they name: `kmeans_id`: for each index of dp, exactly 512 of its 4096 rows have an id in each aligned block of 2048 centroids. `members`: entries past counts[g, s] are 0; the valid entries of all clusters for one index s of dp list each of its 4096 local rows exactly once. For each index of dp the counts sum to 4096; some cluster has 16 valid entries from every index of dp. `owner_groups`: every cluster appears exactly once.
All inputs are finite; a program needn't handle non-finite values.
Results may differ from the reference program's by a relative error of at most 0.0021.
Values may be sent and summed in bfloat16 or wider, within the bound.
A program may use at most 128 MiB of HBM per device.

```python
import jax
import jax.numpy as jnp
from jax import lax

D = 1024
CENT_DEV = 2048
ROW_DEV = 4096
SUB = 16
ROWS = 65536
K = 16384
G_OWN = 4
G = 512
CAP = 256
N_DP = 16
N_CENT = 8


def group_layout(key):
    base_key = jax.random.fold_in(key, 101)
    hot_group = jax.random.randint(jax.random.fold_in(key, 102), (), 0, G, dtype=jnp.int32)
    positions = jnp.arange(G, dtype=jnp.int32)
    class_sizes = jnp.where(positions < G // 4, SUB, jnp.where(positions < G // 2, SUB // 2, SUB // 4)).astype(jnp.int32)
    slot_ids = jnp.arange(SUB, dtype=jnp.int32)

    def per_source(source):
        source_key = jax.random.fold_in(base_key, source)
        key_order, key_rows = jax.random.split(source_key)
        order = jax.random.permutation(key_order, G).astype(jnp.int32)
        where_hot = jnp.argmax(order == hot_group)
        first_entry = order[0]
        order = order.at[where_hot].set(first_entry).at[0].set(hot_group)
        count_table = jnp.zeros((G,), jnp.int32).at[order].set(class_sizes)
        offsets = jnp.cumsum(count_table) - count_table
        row_order = jax.random.permutation(key_rows, ROW_DEV).astype(jnp.int32)
        live_mask = slot_ids[None, :] < count_table[:, None]
        spots = jnp.clip(offsets[:, None] + slot_ids[None, :], 0, ROW_DEV - 1)
        picked = row_order[spots]
        member_table = jnp.where(live_mask, picked, 0).astype(jnp.int32)
        targets = jnp.where(live_mask, picked, ROW_DEV).reshape(-1)
        group_ids = jnp.broadcast_to(positions[:, None], (G, SUB)).reshape(-1)
        group_of = jnp.zeros((ROW_DEV,), jnp.int32).at[targets].set(group_ids, mode='drop')
        return (member_table, count_table, group_of)
    member_table, count_table, group_of = jax.vmap(per_source)(jnp.arange(N_DP, dtype=jnp.int32))
    return (jnp.transpose(member_table, (1, 0, 2)), jnp.transpose(count_table), group_of.reshape(-1))


def family_table(key):
    order = jax.random.permutation(jax.random.fold_in(key, 301), K).astype(jnp.int32)
    return (jnp.argsort(order, stable=True).astype(jnp.int32) % (K // 16)).astype(jnp.int32)


def cluster_ids(key):
    shard_key = jax.random.fold_in(key, 302)

    def per_source(source):
        shuffled = jax.random.permutation(jax.random.fold_in(shard_key, source), ROW_DEV).astype(jnp.int32)
        return shuffled % N_CENT
    shards = jax.vmap(per_source)(jnp.arange(N_DP, dtype=jnp.int32)).reshape(ROWS)
    within = jax.random.randint(jax.random.fold_in(key, 303), (ROWS,), 0, CENT_DEV, dtype=jnp.int32)
    return (shards * CENT_DEV + within).astype(jnp.int32)


def feature_scales(key):
    ramp = 10.0 ** (jnp.arange(D, dtype=jnp.float32) / D)
    return ramp * jax.random.uniform(jax.random.fold_in(key, 204), (D,), jnp.float32, 0.7, 1.4)


def parent_vectors(key):
    return jnp.clip(jax.random.normal(jax.random.fold_in(key, 202), (K // 16, D), jnp.float32), -4.0, 4.0)


def draw_embeddings(key, part):
    member_table, count_table, group_of = group_layout(key)
    group_vectors = jnp.clip(jax.random.normal(jax.random.fold_in(key, 203), (G, D), jnp.float32), -4.0, 4.0)
    row_ids = cluster_ids(key)
    families = family_table(key)
    scales = feature_scales(key)
    noise_key = jax.random.fold_in(key, 205)
    scale_key = jax.random.fold_in(key, 206)
    noise = jnp.clip(jax.random.normal(noise_key, (ROWS, D), jnp.float32), -4.0, 4.0)
    row_scale = 10.0 ** jax.random.uniform(scale_key, (ROWS, 1), jnp.float32, 0.0, 1.0)
    parents = parent_vectors(key)[families[row_ids]]
    mixed = 0.7 * group_vectors[group_of] + 0.7 * parents + 0.5 * noise
    return (row_scale * scales[None, :] * mixed).astype(jnp.bfloat16)


def draw_centroids(key, part):
    row_scale = 10.0 ** jax.random.uniform(jax.random.fold_in(key, 208), (K, 1), jnp.float32, 0.0, 1.0)
    offsets = jnp.clip(jax.random.normal(jax.random.fold_in(key, 209), (K, D), jnp.float32), -4.0, 4.0)
    vectors = parent_vectors(key)[family_table(key)] + 0.8 * offsets
    return (row_scale * feature_scales(key)[None, :] * vectors).astype(jnp.bfloat16)


def draw_kmeans_id(key, part):
    return cluster_ids(key)


def draw_members(key, part):
    return group_layout(key)[0]


def draw_counts(key, part):
    return group_layout(key)[1]


def draw_owner_groups(key, part):
    return jax.random.permutation(jax.random.fold_in(key, 404), G).astype(jnp.int32).reshape(N_DP, N_CENT, G_OWN)


def setup_inputs(seed: int = 0) -> dict:
    seeds = jax.random.split(jax.random.key(seed), 7)
    return {
        "embeddings": draw_embeddings(jax.random.fold_in(seeds[6], 71), 0),
        "centroids": draw_centroids(jax.random.fold_in(seeds[6], 71), 0),
        "kmeans_id": draw_kmeans_id(jax.random.fold_in(seeds[6], 71), 0),
        "members": draw_members(jax.random.fold_in(seeds[6], 71), 0),
        "counts": draw_counts(jax.random.fold_in(seeds[6], 71), 0),
        "owner_groups": draw_owner_groups(jax.random.fold_in(seeds[6], 71), 0),
    }


epsilon = 1e-06

def normalize_rows(values):
    wide = values.astype(jnp.float32)
    return (wide / jnp.sqrt(lax.optimization_barrier(jnp.sum(wide * wide, axis=1, keepdims=True)) + epsilon)).astype(jnp.bfloat16)

def reference(embeddings, centroids, kmeans_id, members, counts, owner_groups):
    unit_rows = normalize_rows(embeddings)
    cent_units = normalize_rows(centroids)

    def block_best(portion):
        return lax.optimization_barrier(jnp.max(jnp.dot(portion, cent_units.T, preferred_element_type=jnp.float32), axis=1))
    best_score = lax.map(block_best, unit_rows.reshape(N_DP, ROW_DEV, D)).reshape(ROWS)
    cent_sums = jax.ops.segment_sum(unit_rows.astype(jnp.float32), kmeans_id, num_segments=K)
    cent_norm = jnp.sqrt(lax.optimization_barrier(jnp.sum(cent_sums * cent_sums, axis=1, keepdims=True)))
    new_centroids = (cent_sums / jnp.maximum(cent_norm, 1.0)).T
    sources = jnp.arange(N_DP, dtype=jnp.int32)[:, None] * ROW_DEV
    slot_ids = jnp.arange(SUB, dtype=jnp.int32)
    diagonal = jnp.arange(CAP)[:, None] == jnp.arange(CAP)[None, :]

    def group_max(group_id):
        row_index = (sources + members[group_id]).reshape(CAP).astype(jnp.int32)
        live_mask = (slot_ids[None, :] < counts[group_id][:, None]).reshape(CAP)
        gathered = unit_rows[row_index]
        similarity = jnp.dot(gathered, gathered.T, preferred_element_type=jnp.float32)
        usable = live_mask[:, None] & live_mask[None, :] & jnp.logical_not(diagonal)
        largest = lax.optimization_barrier(jnp.max(jnp.where(usable, similarity, -jnp.inf), axis=1))
        return jnp.where(jnp.any(usable, axis=1), largest, -1.0)
    slot_max = lax.map(group_max, owner_groups.reshape(-1)).reshape(N_DP, N_CENT, G_OWN, CAP)
    return (best_score, new_centroids, slot_max)
```

```python
import functools

import jax
import jax.numpy as jnp
from jax import lax
from jax.experimental import pallas as pl
from jax.experimental.pallas import tpu as pltpu
from jax.sharding import PartitionSpec as P

EPS = 1e-06
MESH = pl.DeviceIdType.MESH
F32 = jnp.float32
BF16 = jnp.bfloat16
NT = (((1,), (1,)), ((), ()))
NN = (((1,), (0,)), ((), ()))


def dot(a, b, dims):
    return lax.dot_general(a, b, dims, preferred_element_type=F32)


def body(
    og, mem, cnt, ids, emb_hbm, cent_hbm,
    best_out, new_out, slot_out,
    emb, x32, cen, g32, sb, recv, xc, cs, rc, idbuf, rid, rank, sel, ssel,
    tmax, bloc, rbest, acc, ssq, rssq,
    lsem, cl_s, cl_r, ce_s, ce_r, id_s, id_r, sq_s, sq_r, be_s, be_r,
):
    rows, feat = emb.shape
    n_dp, n_cent = 16, 8
    me = lax.axis_index("dp")
    jc = lax.axis_index("cent")
    mx, my = me // 4, lax.rem(me, 4)
    chunk = rows // 8
    share = sel.shape[0]
    cshard = cen.shape[0]
    lo_n = acc.shape[1]
    fpart = feat // n_dp

    def peer(k):
        return lax.rem(mx + k // 4, 4) * 4 + lax.rem(my + lax.rem(k, 4), 4)

    def cpeer(k):
        return lax.rem(jc + k, n_cent)

    slabs = x32.reshape(rows + 1, 8, 128)

    def load(i):
        return pltpu.make_async_copy(
            emb_hbm.at[pl.ds(i * chunk, chunk)], emb.at[pl.ds(i * chunk, chunk)], lsem.at[i]
        )

    cent_load = pltpu.make_async_copy(cent_hbm, cen, lsem.at[8])
    for i in range(8):
        load(i).start()
    cent_load.start()

    barrier = pltpu.get_barrier_semaphore()
    for k in range(1, n_dp):
        pl.semaphore_signal(barrier, inc=1, device_id={"dp": peer(k)}, device_id_type=MESH)
    for k in range(1, n_cent):
        pl.semaphore_signal(barrier, inc=1, device_id={"cent": cpeer(k)}, device_id_type=MESH)

    x32[rows * 8:, :] = jnp.full((8, 128), jnp.nan, F32)

    def widen_chunk(i, _):
        load(i).wait()

        def widen(n, _):
            r = pl.multiple_of(i * chunk + n * 16, 16)
            for c in range(8):
                v = emb[pl.ds(r, 16), c * 128:(c + 1) * 128].astype(F32)
                x32[pl.ds(r * 8 + c, 16, stride=8), :] = v
            return 0

        lax.fori_loop(0, chunk // 16, widen, 0)
        return 0

    lax.fori_loop(0, 8, widen_chunk, 0)
    pl.semaphore_wait(barrier, n_dp + n_cent - 2)

    def gather(t, p, dst):
        g = og[p * 32 + jc * 4 + t]
        live = cnt[g]
        for q in range(16):
            row = jnp.where(q < live, mem[g * 16 + q], rows)
            g32[q * 8:(q + 1) * 8, :] = slabs[row]
        for c in range(8):
            dst[:, c * 128:(c + 1) * 128] = g32[pl.ds(c, 16, stride=8), :].astype(BF16)

    def cl_copy(t, p, s):
        return pltpu.make_async_remote_copy(
            src_ref=sb.at[t, p], dst_ref=recv.at[t, s],
            send_sem=cl_s.at[t, p], recv_sem=cl_r.at[t, s],
            device_id={"dp": p}, device_id_type=MESH,
        )

    def send_round(t):
        def step(k, _):
            p = peer(k)
            gather(t, p, sb.at[t, p])
            cl_copy(t, p, me).start()
            return 0

        lax.fori_loop(1, n_dp, step, 0)
        gather(t, me, recv.at[t, me])

    send_round(0)
    send_round(1)

    idv = ids[...]
    inside = (idv // cshard) == jc
    insf = inside.astype(F32).astype(BF16)
    lane_a = lax.broadcasted_iota(jnp.int32, (128, 128), 0)
    lane_b = lax.broadcasted_iota(jnp.int32, (128, 128), 1)
    upper = (lane_a <= lane_b).astype(F32).astype(BF16)
    run = dot(insf, upper, NN)
    total = dot(insf, jnp.ones((128, 128), BF16), NN).astype(BF16)
    row_a = lax.broadcasted_iota(jnp.int32, (32, 32), 0)
    row_b = lax.broadcasted_iota(jnp.int32, (32, 32), 1)
    lower = (row_b < row_a).astype(F32).astype(BF16)
    before = dot(lower, total, NN)
    rank[0] = jnp.where(inside, before + run - 1.0, -1.0)
    local_id = idv - jc * cshard
    rank[1] = jnp.where(inside, (local_id // 256).astype(F32), 0.0)
    rank[2] = jnp.where(inside, lax.rem(local_id, 256).astype(F32), 0.0)
    xc[...] = jnp.zeros_like(xc)
    ssel[...] = jnp.zeros_like(ssel)
    want = lax.broadcasted_iota(jnp.int32, (share, 128), 0).astype(F32)
    sub16 = lax.broadcasted_iota(jnp.int32, (16, 128), 0)

    def select(n, _):
        for u in range(4):
            q = n * 4 + u
            one = (want == rank[0, pl.ds(q, 1), :]).astype(F32).astype(BF16)
            sel[:, u * 128:(u + 1) * 128] = one
            info = jnp.where(
                sub16 == 0, rank[1, pl.ds(q, 1), :],
                jnp.where(sub16 == 1, rank[2, pl.ds(q, 1), :], 0.0),
            ).astype(BF16)
            ssel[...] += dot(info, one, NT)
        r = pl.multiple_of(n * 512, 512)
        xc[...] += dot(sel[...], emb[pl.ds(r, 512), :], NN)
        return 0

    lax.fori_loop(0, 8, select, 0)
    idbuf[...] = (ssel[0:1, :] * 256.0 + ssel[1:2, :]).astype(jnp.int32)
    rid[me] = idbuf[...]

    def id_copy(p, s):
        return pltpu.make_async_remote_copy(
            src_ref=idbuf, dst_ref=rid.at[s], send_sem=id_s.at[p], recv_sem=id_r.at[s],
            device_id={"dp": p}, device_id_type=MESH,
        )

    def ce_copy(p, s):
        return pltpu.make_async_remote_copy(
            src_ref=cs.at[p], dst_ref=rc.at[s], send_sem=ce_s.at[p], recv_sem=ce_r.at[s],
            device_id={"dp": p}, device_id_type=MESH,
        )

    part = jnp.zeros((share, 128), F32)
    for c in range(8):
        v = xc[:, c * 128:(c + 1) * 128]
        part = part + v * v
    norm = jnp.sqrt(jnp.sum(part, axis=1, keepdims=True) + EPS)
    for c in range(8):
        v = (xc[:, c * 128:(c + 1) * 128] / norm).T.astype(BF16)
        cs[2 * c] = v[:fpart]
        cs[2 * c + 1] = v[fpart:]
    rc[me] = cs[me]

    def send_cent(k, _):
        p = peer(k)
        id_copy(p, me).start()
        ce_copy(p, me).start()
        return 0

    lax.fori_loop(1, n_dp, send_cent, 0)

    send_round(2)
    send_round(3)

    cent_load.wait()

    def unit_cent(n, _):
        r = pl.multiple_of(n * 128, 128)
        v = cen[pl.ds(r, 128), :].astype(F32)
        w = v / jnp.sqrt(jnp.sum(v * v, axis=1, keepdims=True) + EPS)
        cen[pl.ds(r, 128), :] = w.astype(BF16)
        return 0

    lax.fori_loop(0, cshard // 128, unit_cent, 0)

    def score(b, _):
        r = pl.multiple_of(b * 512, 512)

        def tile(n, _):
            k0 = pl.multiple_of(n * 512, 512)
            s = dot(emb[pl.ds(r, 512), :], cen[pl.ds(k0, 512), :], NT)
            m = jnp.maximum(
                jnp.maximum(s[:, 0:128], s[:, 128:256]),
                jnp.maximum(s[:, 256:384], s[:, 384:512]),
            )
            tmax[...] = jnp.where(n == 0, m, jnp.maximum(tmax[...], m))
            return 0

        lax.fori_loop(0, cshard // 512, tile, 0)
        sq = jnp.zeros((512, 128), F32)
        for c in range(8):
            v = emb[pl.ds(r, 512), c * 128:(c + 1) * 128].astype(F32)
            sq = sq + v * v
        top = jnp.max(tmax[...].T, axis=0, keepdims=True)
        nrm = jnp.sqrt(jnp.sum(sq.T, axis=0, keepdims=True) + EPS)
        bloc[pl.ds(b, 1), :] = top / nrm
        return 0

    lax.fori_loop(0, rows // 512, score, 0)

    def be_copy(p, s):
        return pltpu.make_async_remote_copy(
            src_ref=bloc, dst_ref=rbest.at[s], send_sem=be_s.at[p], recv_sem=be_r.at[s],
            device_id={"cent": p}, device_id_type=MESH,
        )

    for k in range(1, n_cent):
        be_copy(cpeer(k), jc).start()

    acc[...] = jnp.zeros_like(acc)
    want_lo = lax.broadcasted_iota(jnp.int32, (lo_n, share), 0)

    def add_rows(s):
        ident = rid[s]
        low = lax.rem(ident, lo_n)
        high = ident // lo_n
        one = (want_lo == low).astype(F32).astype(BF16)
        x = rc[s].astype(F32)
        lhs = jnp.concatenate(
            [(x * (high == h).astype(F32)).astype(BF16) for h in range(cshard // lo_n)], axis=0
        )
        acc[...] += dot(lhs, one, NT)

    def sum_step(k, _):
        s = peer(k)
        id_copy(s, s).wait_recv()
        ce_copy(s, s).wait_recv()
        add_rows(s)
        return 0

    add_rows(me)
    lax.fori_loop(1, n_dp, sum_step, 0)
    for h in range(4):
        a = acc[h * 64:(h + 1) * 64, :]
        q = jnp.sum(a * a, axis=0, keepdims=True)
        ssq[2 * h:2 * h + 1, :] = q[:, :256]
        ssq[2 * h + 1:2 * h + 2, :] = q[:, 256:]

    def sq_copy(p, s):
        return pltpu.make_async_remote_copy(
            src_ref=ssq, dst_ref=rssq.at[s], send_sem=sq_s.at[p], recv_sem=sq_r.at[s],
            device_id={"dp": p}, device_id_type=MESH,
        )

    rssq[me] = ssq[...]

    def send_sq(k, _):
        sq_copy(peer(k), me).start()
        return 0

    lax.fori_loop(1, n_dp, send_sq, 0)

    pa = lax.broadcasted_iota(jnp.int32, (256, 256), 0)
    pb = lax.broadcasted_iota(jnp.int32, (256, 256), 1)
    diag = pa == pb

    def block(t):
        def arrive(k, _):
            s = peer(k)
            cl_copy(t, s, s).wait_recv()
            return 0

        lax.fori_loop(1, n_dp, arrive, 0)
        x = recv[t].reshape(256, feat)
        gm = dot(x, x, NT)
        dg = jnp.where(diag, gm, 0.0)
        icol = 1.0 / jnp.sqrt(jnp.sum(dg, axis=1, keepdims=True) + EPS)
        irow = 1.0 / jnp.sqrt(jnp.sum(dg, axis=0, keepdims=True) + EPS)
        v = gm * icol
        ok = (v == v) & jnp.logical_not(diag)
        m = jnp.max(jnp.where(ok, v, -jnp.inf), axis=0, keepdims=True)
        slot_out[t:t + 1, :] = jnp.where(m > -jnp.inf, m * irow, -1.0)

    block(0)
    block(1)

    def got_sq(k, _):
        s = peer(k)
        sq_copy(s, s).wait_recv()
        return 0

    lax.fori_loop(1, n_dp, got_sq, 0)
    full = rssq[0]
    for s in range(1, n_dp):
        full = full + rssq[s]
    inv = 1.0 / jnp.maximum(jnp.sqrt(full), 1.0)
    for h in range(4):
        for u in range(2):
            lo = u * 256
            new_out[:, h * 512 + lo:h * 512 + lo + 256] = (
                acc[h * 64:(h + 1) * 64, lo:lo + 256] * inv[2 * h + u:2 * h + u + 1, :]
            )

    for k in range(1, n_cent):
        s = cpeer(k)
        be_copy(s, s).wait_recv()
    rbest[jc] = bloc[...]
    top = rbest[0]
    for s in range(1, n_cent):
        top = jnp.maximum(top, rbest[s])
    best_out[...] = top

    block(2)
    block(3)

    def sent(k, _):
        p = peer(k)
        for t in range(4):
            cl_copy(t, p, me).wait_send()
        id_copy(p, me).wait_send()
        ce_copy(p, me).wait_send()
        sq_copy(p, me).wait_send()
        return 0

    lax.fori_loop(1, n_dp, sent, 0)
    for k in range(1, n_cent):
        be_copy(cpeer(k), jc).wait_send()


def shards(embeddings, centroids, kmeans_id, members, counts, owner_groups):
    rows, feat = embeddings.shape
    cshard = centroids.shape[0]
    vm = pl.BlockSpec(memory_space=pltpu.VMEM)
    sm = pl.BlockSpec(memory_space=pltpu.SMEM)
    hbm = pl.BlockSpec(memory_space=pltpu.MemorySpace.HBM)
    dma = pltpu.SemaphoreType.DMA
    best, new, slot = pl.pallas_call(
        body,
        out_shape=(
            jax.ShapeDtypeStruct((8, rows // 8), F32),
            jax.ShapeDtypeStruct((feat // 16, cshard), F32),
            jax.ShapeDtypeStruct((4, 256), F32),
        ),
        in_specs=[sm, sm, sm, vm, hbm, hbm],
        out_specs=(vm, vm, vm),
        scratch_shapes=[
            pltpu.VMEM((rows, feat), BF16),
            pltpu.VMEM((rows * 8 + 8, 128), F32),
            pltpu.VMEM((cshard, feat), BF16),
            pltpu.VMEM((128, 128), F32),
            pltpu.VMEM((4, 16, 16, feat), BF16),
            pltpu.VMEM((4, 16, 16, feat), BF16),
            pltpu.VMEM((512, feat), F32),
            pltpu.VMEM((16, feat // 16, 512), BF16),
            pltpu.VMEM((16, feat // 16, 512), BF16),
            pltpu.VMEM((1, 512), jnp.int32),
            pltpu.VMEM((16, 1, 512), jnp.int32),
            pltpu.VMEM((3, 32, 128), F32),
            pltpu.VMEM((512, 512), BF16),
            pltpu.VMEM((16, 512), F32),
            pltpu.VMEM((512, 128), F32),
            pltpu.VMEM((8, rows // 8), F32),
            pltpu.VMEM((8, 8, rows // 8), F32),
            pltpu.VMEM((256, 512), F32),
            pltpu.VMEM((8, 256), F32),
            pltpu.VMEM((16, 8, 256), F32),
            dma((9,)),
            dma((4, 16)), dma((4, 16)),
            dma((16,)), dma((16,)),
            dma((16,)), dma((16,)),
            dma((16,)), dma((16,)),
            dma((8,)), dma((8,)),
        ],
        compiler_params=pltpu.CompilerParams(
            collective_id=0, has_side_effects=True, vmem_limit_bytes=58 << 20
        ),
        name="window",
    )(
        owner_groups.reshape(-1),
        members.reshape(-1),
        counts.reshape(-1),
        kmeans_id.reshape(32, 128),
        embeddings,
        centroids,
    )
    return best.reshape(rows), new, slot.reshape(1, 1, 4, 256)


def solution(mesh):
    placed = (P("dp", None), P("cent", None), P("dp"), P(None, "dp", None), P(None, "dp"), P())
    return jax.shard_map(
        shards,
        mesh=mesh,
        in_specs=placed,
        out_specs=(P("dp"), P("dp", "cent"), P("dp", "cent", None, None)),
        check_vma=False,
    )
```

```python
import functools

import jax
import jax.numpy as jnp
from jax import lax
from jax.experimental import pallas as pl
from jax.experimental.pallas import tpu as pltpu
from jax.sharding import PartitionSpec as P

EPS = 1e-06
MESH = pl.DeviceIdType.MESH
F32 = jnp.float32
BF16 = jnp.bfloat16
NT = (((1,), (1,)), ((), ()))
NN = (((1,), (0,)), ((), ()))


def dot(a, b, dims):
    return lax.dot_general(a, b, dims, preferred_element_type=F32)


def body(
    og, mem, cnt, ids, emb_hbm, cent_hbm,
    best_out, new_out, slot_out,
    emb, x32, cen, g32, sb, recv, xc, cs, rc, idbuf, rid, rank, sel, info, ssel, hot, lhs,
    tmax, bloc, rbest, acc, ssq, rssq,
    lsem, cl_s, cl_r, ce_s, ce_r, id_s, id_r, sq_s, sq_r, be_s, be_r,
):
    rows, feat = emb.shape
    n_dp, n_cent = 16, 8
    me = lax.axis_index("dp")
    jc = lax.axis_index("cent")
    mx, my = me // 4, lax.rem(me, 4)
    chunk = rows // 8
    share = sel.shape[0]
    cshard = cen.shape[0]
    lo_n = acc.shape[1]
    fpart = feat // n_dp

    def peer(k):
        return lax.rem(mx + k // 4, 4) * 4 + lax.rem(my + lax.rem(k, 4), 4)

    def cpeer(k):
        return lax.rem(jc + k, n_cent)

    slabs = x32.reshape(rows + 1, 8, 128)

    def load(i):
        return pltpu.make_async_copy(
            emb_hbm.at[pl.ds(i * chunk, chunk)], emb.at[pl.ds(i * chunk, chunk)], lsem.at[i]
        )

    cent_load = pltpu.make_async_copy(cent_hbm, cen, lsem.at[8])
    for i in range(8):
        load(i).start()
    cent_load.start()

    barrier = pltpu.get_barrier_semaphore()
    for k in range(1, n_dp):
        pl.semaphore_signal(barrier, inc=1, device_id={"dp": peer(k)}, device_id_type=MESH)
    for k in range(1, n_cent):
        pl.semaphore_signal(barrier, inc=1, device_id={"cent": cpeer(k)}, device_id_type=MESH)

    x32[rows * 8:, :] = jnp.full((8, 128), jnp.nan, F32)

    def widen_chunk(i, _):
        load(i).wait()

        def widen(n, _):
            r = pl.multiple_of(i * chunk + n * 16, 16)
            for c in range(8):
                v = emb[pl.ds(r, 16), c * 128:(c + 1) * 128].astype(F32)
                x32[pl.ds(r * 8 + c, 16, stride=8), :] = v
            return 0

        lax.fori_loop(0, chunk // 16, widen, 0, unroll=4)
        return 0

    lax.fori_loop(0, 8, widen_chunk, 0)
    pl.semaphore_wait(barrier, n_dp + n_cent - 2)

    def gather(t, p, dst):
        g = og[jc, t, p]
        live = cnt[g]
        for q in range(16):
            row = jnp.where(q < live, mem[q, g], rows)
            g32[q * 8:(q + 1) * 8, :] = slabs[row]
        for c in range(8):
            dst[:, c * 128:(c + 1) * 128] = g32[pl.ds(c, 16, stride=8), :].astype(BF16)

    def cl_copy(t, p, s):
        return pltpu.make_async_remote_copy(
            src_ref=sb.at[t, p], dst_ref=recv.at[t, s],
            send_sem=cl_s.at[t, p], recv_sem=cl_r.at[t, s],
            device_id={"dp": p}, device_id_type=MESH,
        )

    def send_round(t):
        def step(k, _):
            p = peer(k)
            gather(t, p, sb.at[t, p])
            cl_copy(t, p, me).start()
            return 0

        lax.fori_loop(1, n_dp, step, 0)
        gather(t, me, recv.at[t, me])

    send_round(0)
    send_round(1)

    idv = ids[...]
    inside = (idv // cshard) == jc
    insf = inside.astype(F32).astype(BF16)
    lane_a = lax.broadcasted_iota(jnp.int32, (128, 128), 0)
    lane_b = lax.broadcasted_iota(jnp.int32, (128, 128), 1)
    upper = (lane_a <= lane_b).astype(F32).astype(BF16)
    run = dot(insf, upper, NN)
    total = dot(insf, jnp.ones((128, 128), BF16), NN).astype(BF16)
    row_a = lax.broadcasted_iota(jnp.int32, (32, 32), 0)
    row_b = lax.broadcasted_iota(jnp.int32, (32, 32), 1)
    lower = (row_b < row_a).astype(F32).astype(BF16)
    before = dot(lower, total, NN)
    rank[0] = jnp.where(inside, before + run - 1.0, -1.0)
    local_id = idv - jc * cshard
    rank[1] = jnp.where(inside, (local_id // 256).astype(F32), 0.0)
    rank[2] = jnp.where(inside, lax.rem(local_id, 256).astype(F32), 0.0)
    want = lax.broadcasted_iota(jnp.int32, (256, 128), 0).astype(F32).astype(BF16)
    sub16 = lax.broadcasted_iota(jnp.int32, (16, 128), 0)
    one_b, zero_b = jnp.ones((256, 128), BF16), jnp.zeros((256, 128), BF16)

    def select(q, _):
        at = pl.ds(pl.multiple_of(q * 128, 128), 128)
        r = rank[0, pl.ds(q, 1), :]
        for u in range(share // 256):
            ru = jnp.broadcast_to((r - u * 256.0).astype(BF16), (256, 128))
            sel[u * 256:(u + 1) * 256, at] = jnp.where(want == ru, one_b, zero_b)
        info[:, at] = jnp.where(
            sub16 == 0, rank[1, pl.ds(q, 1), :],
            jnp.where(sub16 == 1, rank[2, pl.ds(q, 1), :], 0.0),
        ).astype(BF16)
        return 0

    lax.fori_loop(0, rows // 128, select, 0, unroll=4)
    ssel[...] = dot(info[...], sel[...], NT)
    xc[...] = dot(sel[...], emb[...], NN)
    idbuf[...] = (ssel[0:1, :] * 256.0 + ssel[1:2, :]).astype(jnp.int32)
    rid[me] = idbuf[...]

    def id_copy(p, s):
        return pltpu.make_async_remote_copy(
            src_ref=idbuf, dst_ref=rid.at[s], send_sem=id_s.at[p], recv_sem=id_r.at[s],
            device_id={"dp": p}, device_id_type=MESH,
        )

    def ce_copy(p, s):
        return pltpu.make_async_remote_copy(
            src_ref=cs.at[p], dst_ref=rc.at[s], send_sem=ce_s.at[p], recv_sem=ce_r.at[s],
            device_id={"dp": p}, device_id_type=MESH,
        )

    part = jnp.zeros((share, 128), F32)
    for c in range(8):
        v = xc[:, c * 128:(c + 1) * 128]
        part = part + v * v
    scale = 1.0 / jnp.sqrt(jnp.sum(part, axis=1, keepdims=True) + EPS)
    for c in range(8):
        v = (xc[:, c * 128:(c + 1) * 128] * scale).astype(BF16).T
        cs[2 * c] = v[:fpart]
        cs[2 * c + 1] = v[fpart:]
    rc[me] = cs[me]

    def send_cent(k, _):
        p = peer(k)
        id_copy(p, me).start()
        ce_copy(p, me).start()
        return 0

    lax.fori_loop(1, n_dp, send_cent, 0)

    send_round(2)
    send_round(3)

    cent_load.wait()

    def unit_cent(n, _):
        r = pl.multiple_of(n * 128, 128)
        v = cen[pl.ds(r, 128), :].astype(F32)
        w = v * (1.0 / jnp.sqrt(jnp.sum(v * v, axis=1, keepdims=True) + EPS))
        cen[pl.ds(r, 128), :] = w.astype(BF16)
        return 0

    lax.fori_loop(0, cshard // 128, unit_cent, 0)

    blk = tmax.shape[0]

    def score(b, _):
        r = pl.multiple_of(b * blk, blk)

        def tile(n, _):
            k0 = pl.multiple_of(n * blk, blk)
            s = dot(emb[pl.ds(r, blk), :], cen[pl.ds(k0, blk), :], NT)
            m = s[:, 0:128]
            for c in range(1, blk // 128):
                m = jnp.maximum(m, s[:, c * 128:(c + 1) * 128])
            tmax[...] = jnp.where(n == 0, m, jnp.maximum(tmax[...], m))
            return 0

        lax.fori_loop(0, cshard // blk, tile, 0)
        sq = jnp.zeros((blk, 128), F32)
        for c in range(8):
            v = emb[pl.ds(r, blk), c * 128:(c + 1) * 128].astype(F32)
            sq = sq + v * v
        top = jnp.max(tmax[...].T, axis=0, keepdims=True)
        nrm = jnp.sqrt(jnp.sum(sq.T, axis=0, keepdims=True) + EPS)
        top = top / nrm
        for c in range(blk // 128):
            bloc[pl.ds(b * (blk // 128) + c, 1), :] = top[:, c * 128:(c + 1) * 128]
        return 0

    lax.fori_loop(0, rows // blk, score, 0)

    def be_copy(p, s):
        return pltpu.make_async_remote_copy(
            src_ref=bloc, dst_ref=rbest.at[s], send_sem=be_s.at[p], recv_sem=be_r.at[s],
            device_id={"cent": p}, device_id_type=MESH,
        )

    for k in range(1, n_cent):
        be_copy(cpeer(k), jc).start()

    n_hi = cshard // lo_n
    want_lo = lax.broadcasted_iota(jnp.int32, (lo_n, share), 0).astype(F32).astype(BF16)
    one_s, zero_s = jnp.ones((lo_n, share), BF16), jnp.zeros((lo_n, share), BF16)
    zero_f = jnp.zeros((fpart, share), BF16)

    def place(s, u):
        ident = rid[s]
        low = (ident & (lo_n - 1)).astype(F32).astype(BF16)
        high = (ident // lo_n).astype(F32).astype(BF16)
        at = slice(u * share, (u + 1) * share)
        hot[:, at] = jnp.where(want_lo == jnp.broadcast_to(low, (lo_n, share)), one_s, zero_s)
        x = rc[s]
        hb = jnp.broadcast_to(high, (fpart, share))
        for h in range(n_hi):
            lhs[h * fpart:(h + 1) * fpart, at] = jnp.where(hb == float(h), x, zero_f)

    for k in range(n_dp):
        s = peer(k)
        if k > 0:
            id_copy(s, s).wait_recv()
            ce_copy(s, s).wait_recv()
        place(s, k % 4)
        if k % 4 == 3:
            add = dot(lhs[...], hot[...], NT)
            acc[...] = add if k == 3 else acc[...] + add
    for h in range(n_hi):
        a = acc[h * fpart:(h + 1) * fpart, :]
        ssq[h:h + 1, :] = jnp.sum(a * a, axis=0, keepdims=True)

    def sq_copy(p, s):
        return pltpu.make_async_remote_copy(
            src_ref=ssq, dst_ref=rssq.at[s], send_sem=sq_s.at[p], recv_sem=sq_r.at[s],
            device_id={"dp": p}, device_id_type=MESH,
        )

    rssq[me] = ssq[...]

    def send_sq(k, _):
        sq_copy(peer(k), me).start()
        return 0

    lax.fori_loop(1, n_dp, send_sq, 0)

    pa = lax.broadcasted_iota(jnp.int32, (256, 256), 0)
    pb = lax.broadcasted_iota(jnp.int32, (256, 256), 1)
    diag = pa == pb

    def block(t):
        def arrive(k, _):
            s = peer(k)
            cl_copy(t, s, s).wait_recv()
            return 0

        lax.fori_loop(1, n_dp, arrive, 0)
        x = recv[t].reshape(256, feat)
        gm = dot(x, x, NT)
        dg = jnp.where(diag, gm, 0.0)
        icol = 1.0 / jnp.sqrt(jnp.sum(dg, axis=1, keepdims=True) + EPS)
        irow = 1.0 / jnp.sqrt(jnp.sum(dg, axis=0, keepdims=True) + EPS)
        v = gm * icol
        ok = (v == v) & jnp.logical_not(diag)
        m = jnp.max(jnp.where(ok, v, -jnp.inf), axis=0, keepdims=True)
        slot_out[t:t + 1, :] = jnp.where(m > -jnp.inf, m * irow, -1.0)

    block(0)
    block(1)

    def got_sq(k, _):
        s = peer(k)
        sq_copy(s, s).wait_recv()
        return 0

    lax.fori_loop(1, n_dp, got_sq, 0)
    full = rssq[0]
    for s in range(1, n_dp):
        full = full + rssq[s]
    inv = 1.0 / jnp.maximum(jnp.sqrt(full), 1.0)
    for h in range(n_hi):
        new_out[:, h * lo_n:(h + 1) * lo_n] = (
            acc[h * fpart:(h + 1) * fpart, :] * inv[h:h + 1, :]
        )

    for k in range(1, n_cent):
        s = cpeer(k)
        be_copy(s, s).wait_recv()
    rbest[jc] = bloc[...]
    top = rbest[0]
    for s in range(1, n_cent):
        top = jnp.maximum(top, rbest[s])
    best_out[...] = top

    block(2)
    block(3)

    def sent(k, _):
        p = peer(k)
        for t in range(4):
            cl_copy(t, p, me).wait_send()
        id_copy(p, me).wait_send()
        ce_copy(p, me).wait_send()
        sq_copy(p, me).wait_send()
        return 0

    lax.fori_loop(1, n_dp, sent, 0)
    for k in range(1, n_cent):
        be_copy(cpeer(k), jc).wait_send()


def hand_over(best, new, slot, best_out, new_out, slot_out, sems):
    pairs = ((new, new_out), (best, best_out), (slot, slot_out))
    copies = [pltpu.make_async_copy(a, b, sems.at[i]) for i, (a, b) in enumerate(pairs)]
    for c in copies:
        c.start()
    for c in copies:
        c.wait()


def shards(embeddings, centroids, kmeans_id, members, counts, owner_groups):
    rows, feat = embeddings.shape
    cshard = centroids.shape[0]
    vm = pl.BlockSpec(memory_space=pltpu.VMEM)
    sm = pl.BlockSpec(memory_space=pltpu.SMEM)
    hbm = pl.BlockSpec(memory_space=pltpu.MemorySpace.HBM)
    dma = pltpu.SemaphoreType.DMA
    best, new, slot = pl.pallas_call(
        body,
        out_shape=(
            jax.ShapeDtypeStruct((rows // 128, 128), F32),
            jax.ShapeDtypeStruct((feat // 16, cshard), F32),
            jax.ShapeDtypeStruct((4, 256), F32),
        ),
        in_specs=[sm, sm, sm, vm, hbm, hbm],
        out_specs=(vm, vm, vm),
        scratch_shapes=[
            pltpu.VMEM((rows, feat), BF16),
            pltpu.VMEM((rows * 8 + 8, 128), F32),
            pltpu.VMEM((cshard, feat), BF16),
            pltpu.VMEM((128, 128), F32),
            pltpu.VMEM((4, 16, 16, feat), BF16),
            pltpu.VMEM((4, 16, 16, feat), BF16),
            pltpu.VMEM((512, feat), F32),
            pltpu.VMEM((16, feat // 16, 512), BF16),
            pltpu.VMEM((16, feat // 16, 512), BF16),
            pltpu.VMEM((1, 512), jnp.int32),
            pltpu.VMEM((16, 1, 512), jnp.int32),
            pltpu.VMEM((3, 32, 128), F32),
            pltpu.VMEM((512, rows), BF16),
            pltpu.VMEM((16, rows), BF16),
            pltpu.VMEM((16, 512), F32),
            pltpu.VMEM((256, 2048), BF16),
            pltpu.VMEM((512, 2048), BF16),
            pltpu.VMEM((1024, 128), F32),
            pltpu.VMEM((rows // 128, 128), F32),
            pltpu.VMEM((8, rows // 128, 128), F32),
            pltpu.VMEM((512, 256), F32),
            pltpu.VMEM((8, 256), F32),
            pltpu.VMEM((16, 8, 256), F32),
            dma((9,)),
            dma((4, 16)), dma((4, 16)),
            dma((16,)), dma((16,)),
            dma((16,)), dma((16,)),
            dma((16,)), dma((16,)),
            dma((8,)), dma((8,)),
        ],
        compiler_params=pltpu.CompilerParams(
            collective_id=0, has_side_effects=True, vmem_limit_bytes=58 << 20
        ),
        name="window",
    )(
        owner_groups.transpose(1, 2, 0),
        members[:, 0, :].T,
        counts.reshape(-1),
        kmeans_id.reshape(32, 128),
        embeddings,
        centroids,
    )
    best, new, slot = pl.pallas_call(
        hand_over,
        out_shape=tuple(jax.ShapeDtypeStruct(v.shape, v.dtype) for v in (best, new, slot)),
        in_specs=[hbm, hbm, hbm],
        out_specs=(hbm, hbm, hbm),
        scratch_shapes=[dma((3,))],
        name="hand_over",
    )(best, new, slot)
    return best.reshape(rows), new, slot.reshape(1, 1, 4, 256)


def solution(mesh):
    placed = (P("dp", None), P("cent", None), P("dp"), P(None, "dp", None), P(None, "dp"), P())
    return jax.shard_map(
        shards,
        mesh=mesh,
        in_specs=placed,
        out_specs=(P("dp"), P("dp", "cent"), P("dp", "cent", None, None)),
        check_vma=False,
    )
```

```python
import functools

import jax
import jax.numpy as jnp
from jax import lax
from jax.experimental import pallas as pl
from jax.experimental.pallas import tpu as pltpu
from jax.sharding import PartitionSpec as P

EPS = 1e-06
MESH = pl.DeviceIdType.MESH
F32 = jnp.float32
BF16 = jnp.bfloat16
NT = (((1,), (1,)), ((), ()))
NN = (((1,), (0,)), ((), ()))


def dot(a, b, dims):
    return lax.dot_general(a, b, dims, preferred_element_type=F32)


def body(
    og, mem, cnt, ids, emb_hbm, cent_hbm,
    best_out, new_out, slot_out,
    emb, x32, cen, g32, sb, recv, xc, cs, rc, idbuf, rid, rank, sel, info, ssel, hot, lhs,
    tmax, bloc, rbest, acc, ssq, rssq,
    lsem, cl_s, cl_r, ce_s, ce_r, id_s, id_r, sq_s, sq_r, be_s, be_r,
):
    rows, feat = emb.shape
    n_dp, n_cent = 16, 8
    me = lax.axis_index("dp")
    jc = lax.axis_index("cent")
    mx, my = me // 4, lax.rem(me, 4)
    chunk = rows // 8
    share = sel.shape[0]
    cshard = cen.shape[0]
    lo_n = acc.shape[1]
    fpart = feat // n_dp

    def peer(k):
        return lax.rem(mx + k // 4, 4) * 4 + lax.rem(my + lax.rem(k, 4), 4)

    def cpeer(k):
        return lax.rem(jc + k, n_cent)

    slabs = x32.reshape(rows + 1, 8, 128)

    def load(i):
        return pltpu.make_async_copy(
            emb_hbm.at[pl.ds(i * chunk, chunk)], emb.at[pl.ds(i * chunk, chunk)], lsem.at[i]
        )

    cent_load = pltpu.make_async_copy(cent_hbm, cen, lsem.at[8])
    for i in range(8):
        load(i).start()
    cent_load.start()

    barrier = pltpu.get_barrier_semaphore()
    for k in range(1, n_dp):
        pl.semaphore_signal(barrier, inc=1, device_id={"dp": peer(k)}, device_id_type=MESH)
    for k in range(1, n_cent):
        pl.semaphore_signal(barrier, inc=1, device_id={"cent": cpeer(k)}, device_id_type=MESH)

    x32[rows * 8:, :] = jnp.full((8, 128), jnp.nan, F32)

    def widen_chunk(i, _):
        load(i).wait()

        def widen(n, _):
            r = pl.multiple_of(i * chunk + n * 16, 16)
            for c in range(8):
                v = emb[pl.ds(r, 16), c * 128:(c + 1) * 128].astype(F32)
                x32[pl.ds(r * 8 + c, 16, stride=8), :] = v
            return 0

        lax.fori_loop(0, chunk // 16, widen, 0, unroll=4)
        return 0

    lax.fori_loop(0, 8, widen_chunk, 0)
    pl.semaphore_wait(barrier, n_dp + n_cent - 2)

    def gather(t, p, dst):
        g = og[jc, t, p]
        live = cnt[g]
        for q in range(16):
            row = jnp.where(q < live, mem[q, g], rows)
            g32[q * 8:(q + 1) * 8, :] = slabs[row]
        for c in range(8):
            dst[:, c * 128:(c + 1) * 128] = g32[pl.ds(c, 16, stride=8), :].astype(BF16)

    def cl_copy(t, p, s):
        return pltpu.make_async_remote_copy(
            src_ref=sb.at[t, p], dst_ref=recv.at[t, s],
            send_sem=cl_s.at[t, p], recv_sem=cl_r.at[t, s],
            device_id={"dp": p}, device_id_type=MESH,
        )

    def send_round(t):
        def step(k, _):
            p = peer(k)
            gather(t, p, sb.at[t, p])
            cl_copy(t, p, me).start()
            return 0

        lax.fori_loop(1, n_dp, step, 0)
        gather(t, me, recv.at[t, me])

    send_round(0)
    send_round(1)

    idv = ids[...]
    inside = (idv // cshard) == jc
    insf = inside.astype(F32).astype(BF16)
    lane_a = lax.broadcasted_iota(jnp.int32, (128, 128), 0)
    lane_b = lax.broadcasted_iota(jnp.int32, (128, 128), 1)
    upper = (lane_a <= lane_b).astype(F32).astype(BF16)
    run = dot(insf, upper, NN)
    total = dot(insf, jnp.ones((128, 128), BF16), NN).astype(BF16)
    row_a = lax.broadcasted_iota(jnp.int32, (32, 32), 0)
    row_b = lax.broadcasted_iota(jnp.int32, (32, 32), 1)
    lower = (row_b < row_a).astype(F32).astype(BF16)
    before = dot(lower, total, NN)
    rank[0] = jnp.where(inside, before + run - 1.0, -1.0)
    local_id = idv - jc * cshard
    rank[1] = jnp.where(inside, (local_id // 256).astype(F32), 0.0)
    rank[2] = jnp.where(inside, lax.rem(local_id, 256).astype(F32), 0.0)
    want = lax.broadcasted_iota(jnp.int32, (256, 128), 0).astype(F32).astype(BF16)
    sub16 = lax.broadcasted_iota(jnp.int32, (16, 128), 0)
    one_b, zero_b = jnp.ones((256, 128), BF16), jnp.zeros((256, 128), BF16)

    def select(q, _):
        at = pl.ds(pl.multiple_of(q * 128, 128), 128)
        r = rank[0, pl.ds(q, 1), :]
        for u in range(share // 256):
            ru = jnp.broadcast_to((r - u * 256.0).astype(BF16), (256, 128))
            sel[u * 256:(u + 1) * 256, at] = jnp.where(want == ru, one_b, zero_b)
        info[:, at] = jnp.where(
            sub16 == 0, rank[1, pl.ds(q, 1), :],
            jnp.where(sub16 == 1, rank[2, pl.ds(q, 1), :], 0.0),
        ).astype(BF16)
        return 0

    lax.fori_loop(0, rows // 128, select, 0, unroll=4)
    ssel[...] = dot(info[...], sel[...], NT)
    xc[...] = dot(sel[...], emb[...], NN)
    idbuf[...] = (ssel[0:1, :] * 256.0 + ssel[1:2, :]).astype(jnp.int32)
    rid[me] = idbuf[...]

    def id_copy(p, s):
        return pltpu.make_async_remote_copy(
            src_ref=idbuf, dst_ref=rid.at[s], send_sem=id_s.at[p], recv_sem=id_r.at[s],
            device_id={"dp": p}, device_id_type=MESH,
        )

    def ce_copy(p, s):
        return pltpu.make_async_remote_copy(
            src_ref=cs.at[p], dst_ref=rc.at[s], send_sem=ce_s.at[p], recv_sem=ce_r.at[s],
            device_id={"dp": p}, device_id_type=MESH,
        )

    part = jnp.zeros((share, 128), F32)
    for c in range(8):
        v = xc[:, c * 128:(c + 1) * 128]
        part = part + v * v
    scale = 1.0 / jnp.sqrt(jnp.sum(part, axis=1, keepdims=True) + EPS)
    for c in range(8):
        v = (xc[:, c * 128:(c + 1) * 128] * scale).astype(BF16).T
        cs[2 * c] = v[:fpart]
        cs[2 * c + 1] = v[fpart:]
    rc[me] = cs[me]

    def send_cent(k, _):
        p = peer(k)
        id_copy(p, me).start()
        ce_copy(p, me).start()
        return 0

    lax.fori_loop(1, n_dp, send_cent, 0)

    send_round(2)
    send_round(3)

    cent_load.wait()

    def unit_cent(n, _):
        r = pl.multiple_of(n * 128, 128)
        v = cen[pl.ds(r, 128), :].astype(F32)
        w = v * (1.0 / jnp.sqrt(jnp.sum(v * v, axis=1, keepdims=True) + EPS))
        cen[pl.ds(r, 128), :] = w.astype(BF16)
        return 0

    lax.fori_loop(0, cshard // 128, unit_cent, 0)

    blk = tmax.shape[0]

    def score(b, _):
        r = pl.multiple_of(b * blk, blk)

        def tile(n, _):
            k0 = pl.multiple_of(n * blk, blk)
            s = dot(emb[pl.ds(r, blk), :], cen[pl.ds(k0, blk), :], NT)
            m = s[:, 0:128]
            for c in range(1, blk // 128):
                m = jnp.maximum(m, s[:, c * 128:(c + 1) * 128])
            tmax[...] = jnp.where(n == 0, m, jnp.maximum(tmax[...], m))
            return 0

        lax.fori_loop(0, cshard // blk, tile, 0)
        sq = jnp.zeros((blk, 128), F32)
        for c in range(8):
            v = emb[pl.ds(r, blk), c * 128:(c + 1) * 128].astype(F32)
            sq = sq + v * v
        top = jnp.max(tmax[...].T, axis=0, keepdims=True)
        nrm = jnp.sqrt(jnp.sum(sq.T, axis=0, keepdims=True) + EPS)
        top = top / nrm
        for c in range(blk // 128):
            bloc[pl.ds(b * (blk // 128) + c, 1), :] = top[:, c * 128:(c + 1) * 128]
        return 0

    lax.fori_loop(0, rows // blk, score, 0)

    def be_copy(p, s):
        return pltpu.make_async_remote_copy(
            src_ref=bloc, dst_ref=rbest.at[s], send_sem=be_s.at[p], recv_sem=be_r.at[s],
            device_id={"cent": p}, device_id_type=MESH,
        )

    for k in range(1, n_cent):
        be_copy(cpeer(k), jc).start()

    n_hi = cshard // lo_n
    want_lo = lax.broadcasted_iota(jnp.int32, (lo_n, share), 0).astype(F32).astype(BF16)
    one_s, zero_s = jnp.ones((lo_n, share), BF16), jnp.zeros((lo_n, share), BF16)
    zero_f = jnp.zeros((fpart, share), BF16)

    def place(s, u):
        ident = rid[s]
        low = (ident & (lo_n - 1)).astype(F32).astype(BF16)
        high = (ident // lo_n).astype(F32).astype(BF16)
        at = slice(u * share, (u + 1) * share)
        hot[:, at] = jnp.where(want_lo == jnp.broadcast_to(low, (lo_n, share)), one_s, zero_s)
        x = rc[s]
        hb = jnp.broadcast_to(high, (fpart, share))
        for h in range(n_hi):
            lhs[h * fpart:(h + 1) * fpart, at] = jnp.where(hb == float(h), x, zero_f)

    for k in range(n_dp):
        s = peer(k)
        if k > 0:
            id_copy(s, s).wait_recv()
            ce_copy(s, s).wait_recv()
        place(s, k % 4)
        if k % 4 == 3:
            add = dot(lhs[...], hot[...], NT)
            acc[...] = add if k == 3 else acc[...] + add
    for h in range(n_hi):
        a = acc[h * fpart:(h + 1) * fpart, :]
        ssq[h:h + 1, :] = jnp.sum(a * a, axis=0, keepdims=True)

    def sq_copy(p, s):
        return pltpu.make_async_remote_copy(
            src_ref=ssq, dst_ref=rssq.at[s], send_sem=sq_s.at[p], recv_sem=sq_r.at[s],
            device_id={"dp": p}, device_id_type=MESH,
        )

    rssq[me] = ssq[...]

    def send_sq(k, _):
        sq_copy(peer(k), me).start()
        return 0

    lax.fori_loop(1, n_dp, send_sq, 0)

    pa = lax.broadcasted_iota(jnp.int32, (256, 256), 0)
    pb = lax.broadcasted_iota(jnp.int32, (256, 256), 1)
    diag = pa == pb

    def block(t):
        def arrive(k, _):
            s = peer(k)
            cl_copy(t, s, s).wait_recv()
            return 0

        lax.fori_loop(1, n_dp, arrive, 0)
        x = recv[t].reshape(256, feat)
        gm = dot(x, x, NT)
        dg = jnp.where(diag, gm, 0.0)
        icol = 1.0 / jnp.sqrt(jnp.sum(dg, axis=1, keepdims=True) + EPS)
        irow = 1.0 / jnp.sqrt(jnp.sum(dg, axis=0, keepdims=True) + EPS)
        v = gm * icol
        ok = (v == v) & jnp.logical_not(diag)
        m = jnp.max(jnp.where(ok, v, -jnp.inf), axis=0, keepdims=True)
        slot_out[t:t + 1, :] = jnp.where(m > -jnp.inf, m * irow, -1.0)

    block(0)
    block(1)

    def got_sq(k, _):
        s = peer(k)
        sq_copy(s, s).wait_recv()
        return 0

    lax.fori_loop(1, n_dp, got_sq, 0)
    full = rssq[0]
    for s in range(1, n_dp):
        full = full + rssq[s]
    inv = 1.0 / jnp.maximum(jnp.sqrt(full), 1.0)
    for h in range(n_hi):
        new_out[:, h * lo_n:(h + 1) * lo_n] = (
            acc[h * fpart:(h + 1) * fpart, :] * inv[h:h + 1, :]
        )

    for k in range(1, n_cent):
        s = cpeer(k)
        be_copy(s, s).wait_recv()
    rbest[jc] = bloc[...]
    top = rbest[0]
    for s in range(1, n_cent):
        top = jnp.maximum(top, rbest[s])
    best_out[...] = top

    block(2)
    block(3)

    def sent(k, _):
        p = peer(k)
        for t in range(4):
            cl_copy(t, p, me).wait_send()
        id_copy(p, me).wait_send()
        ce_copy(p, me).wait_send()
        sq_copy(p, me).wait_send()
        return 0

    lax.fori_loop(1, n_dp, sent, 0)
    for k in range(1, n_cent):
        be_copy(cpeer(k), jc).wait_send()


def hand_over(best, new, slot, best_out, new_out, slot_out):
    best_out[...] = best[...]
    new_out[...] = new[...]
    slot_out[...] = slot[...]


def shards(embeddings, centroids, kmeans_id, members, counts, owner_groups):
    rows, feat = embeddings.shape
    cshard = centroids.shape[0]
    vm = pl.BlockSpec(memory_space=pltpu.VMEM)
    sm = pl.BlockSpec(memory_space=pltpu.SMEM)
    hbm = pl.BlockSpec(memory_space=pltpu.MemorySpace.HBM)
    dma = pltpu.SemaphoreType.DMA
    best, new, slot = pl.pallas_call(
        body,
        out_shape=(
            jax.ShapeDtypeStruct((rows // 128, 128), F32),
            jax.ShapeDtypeStruct((feat // 16, cshard), F32),
            jax.ShapeDtypeStruct((4, 256), F32),
        ),
        in_specs=[sm, sm, sm, vm, hbm, hbm],
        out_specs=(vm, vm, vm),
        scratch_shapes=[
            pltpu.VMEM((rows, feat), BF16),
            pltpu.VMEM((rows * 8 + 8, 128), F32),
            pltpu.VMEM((cshard, feat), BF16),
            pltpu.VMEM((128, 128), F32),
            pltpu.VMEM((4, 16, 16, feat), BF16),
            pltpu.VMEM((4, 16, 16, feat), BF16),
            pltpu.VMEM((512, feat), F32),
            pltpu.VMEM((16, feat // 16, 512), BF16),
            pltpu.VMEM((16, feat // 16, 512), BF16),
            pltpu.VMEM((1, 512), jnp.int32),
            pltpu.VMEM((16, 1, 512), jnp.int32),
            pltpu.VMEM((3, 32, 128), F32),
            pltpu.VMEM((512, rows), BF16),
            pltpu.VMEM((16, rows), BF16),
            pltpu.VMEM((16, 512), F32),
            pltpu.VMEM((256, 2048), BF16),
            pltpu.VMEM((512, 2048), BF16),
            pltpu.VMEM((1024, 128), F32),
            pltpu.VMEM((rows // 128, 128), F32),
            pltpu.VMEM((8, rows // 128, 128), F32),
            pltpu.VMEM((512, 256), F32),
            pltpu.VMEM((8, 256), F32),
            pltpu.VMEM((16, 8, 256), F32),
            dma((9,)),
            dma((4, 16)), dma((4, 16)),
            dma((16,)), dma((16,)),
            dma((16,)), dma((16,)),
            dma((16,)), dma((16,)),
            dma((8,)), dma((8,)),
        ],
        compiler_params=pltpu.CompilerParams(
            collective_id=0, has_side_effects=True, vmem_limit_bytes=58 << 20
        ),
        name="window",
    )(
        owner_groups.transpose(1, 2, 0),
        members[:, 0, :].T,
        counts.reshape(-1),
        kmeans_id.reshape(32, 128),
        embeddings,
        centroids,
    )
    best, new, slot = pl.pallas_call(
        hand_over,
        out_shape=tuple(jax.ShapeDtypeStruct(v.shape, v.dtype) for v in (best, new, slot)),
        in_specs=[vm, vm, vm],
        out_specs=(vm, vm, vm),
        compiler_params=pltpu.CompilerParams(vmem_limit_bytes=4 << 20),
        name="hand_over",
    )(best, new, slot)
    return best.reshape(rows), new, slot.reshape(1, 1, 4, 256)


def solution(mesh):
    placed = (P("dp", None), P("cent", None), P("dp"), P(None, "dp", None), P(None, "dp"), P())
    return jax.shard_map(
        shards,
        mesh=mesh,
        in_specs=placed,
        out_specs=(P("dp"), P("dp", "cent"), P("dp", "cent", None, None)),
        check_vma=False,
    )
```

```python
import functools

import jax
import jax.numpy as jnp
from jax import lax
from jax.experimental import pallas as pl
from jax.experimental.pallas import tpu as pltpu
from jax.sharding import PartitionSpec as P

EPS = 1e-06
MESH = pl.DeviceIdType.MESH
F32 = jnp.float32
BF16 = jnp.bfloat16
NT = (((1,), (1,)), ((), ()))
NN = (((1,), (0,)), ((), ()))


def dot(a, b, dims):
    return lax.dot_general(a, b, dims, preferred_element_type=F32)


def body(
    og_hbm, mem_hbm, cnt_hbm, ids_hbm, emb_hbm, cent_hbm,
    best_out, new_out, slot_out,
    og, mem, cnt, ids, pick, emb, x32, sqp, cen, g32, sb, recv, xc, cs, rc, idbuf, lbuf, rid, rank, sel, info, ssel, hot, lhs,
    tmax, bloc, rbest, acc, ssq, rssq,
    lsem, cl_s, cl_r, ce_s, ce_r, id_s, id_r, sq_s, sq_r, be_s, be_r,
):
    rows, feat = emb.shape
    n_dp, n_cent = 16, 8
    me = lax.axis_index("dp")
    jc = lax.axis_index("cent")
    mx, my = me // 4, lax.rem(me, 4)
    chunk = rows // 8
    share = pick.shape[1]
    cshard = cen.shape[0]
    lo_n = acc.shape[1]
    fpart = feat // n_dp

    def peer(k):
        return lax.rem(mx + k // 4, 4) * 4 + lax.rem(my + lax.rem(k, 4), 4)

    def cpeer(k):
        return lax.rem(jc + k, n_cent)

    slabs = x32.reshape(rows + 1, 8, 128)

    def load(i):
        return pltpu.make_async_copy(
            emb_hbm.at[pl.ds(i * chunk, chunk)], emb.at[pl.ds(i * chunk, chunk)], lsem.at[i]
        )

    cent_load = pltpu.make_async_copy(cent_hbm, cen, lsem.at[8])
    tables = [
        pltpu.make_async_copy(a, b, lsem.at[9 + i])
        for i, (a, b) in enumerate(((og_hbm, og), (mem_hbm, mem), (cnt_hbm, cnt), (ids_hbm, ids)))
    ]
    for c in tables:
        c.start()
    for i in range(8):
        load(i).start()

    barrier = pltpu.get_barrier_semaphore()
    for k in range(1, n_dp):
        pl.semaphore_signal(barrier, inc=1, device_id={"dp": peer(k)}, device_id_type=MESH)
    for k in range(1, n_cent):
        pl.semaphore_signal(barrier, inc=1, device_id={"cent": cpeer(k)}, device_id_type=MESH)

    x32[rows * 8:, :] = jnp.full((8, 128), jnp.nan, F32)

    def widen_chunk(i, _):
        load(i).wait()

        def widen(n, _):
            r = pl.multiple_of(i * chunk + n * 16, 16)
            square = jnp.zeros((16, 128), F32)
            for c in range(8):
                v = emb[pl.ds(r, 16), c * 128:(c + 1) * 128].astype(F32)
                x32[pl.ds(r * 8 + c, 16, stride=8), :] = v
                square = square + v * v
            sqp[pl.ds(r, 16), :] = square
            return 0

        lax.fori_loop(0, chunk // 16, widen, 0, unroll=4)
        return 0

    lax.fori_loop(0, 8, widen_chunk, 0)
    cent_load.start()
    for c in tables:
        c.wait()
    pl.semaphore_wait(barrier, n_dp + n_cent - 2)

    def gather(t, p, dst):
        g = og[jc, t, p]
        live = cnt[g]
        for q in range(16):
            row = jnp.where(q < live, mem[q, g], rows)
            g32[q * 8:(q + 1) * 8, :] = slabs[row]
        for c in range(8):
            dst[:, c * 128:(c + 1) * 128] = g32[pl.ds(c, 16, stride=8), :].astype(BF16)

    def cl_copy(t, p, s):
        return pltpu.make_async_remote_copy(
            src_ref=sb.at[t, p], dst_ref=recv.at[t, s],
            send_sem=cl_s.at[t, p], recv_sem=cl_r.at[t, s],
            device_id={"dp": p}, device_id_type=MESH,
        )

    def send_round(t):
        def step(k, _):
            p = peer(k)
            gather(t, p, sb.at[t, p])

            @pl.when(k > 0)
            def _():
                cl_copy(t, p, me).start()

            return 0

        lax.fori_loop(0, n_dp, step, 0)
        recv[t, me] = sb[t, me]

    send_round(0)

    idv = ids[...]
    inside = (idv // cshard) == jc
    insf = inside.astype(F32).astype(BF16)
    lane_a = lax.broadcasted_iota(jnp.int32, (128, 128), 0)
    lane_b = lax.broadcasted_iota(jnp.int32, (128, 128), 1)
    upper = (lane_a <= lane_b).astype(F32).astype(BF16)
    run = dot(insf, upper, NN)
    total = dot(insf, jnp.ones((128, 128), BF16), NN).astype(BF16)
    row_a = lax.broadcasted_iota(jnp.int32, (32, 32), 0)
    row_b = lax.broadcasted_iota(jnp.int32, (32, 32), 1)
    lower = (row_b < row_a).astype(F32).astype(BF16)
    before = dot(lower, total, NN)
    rank[0] = jnp.where(inside, before + run - 1.0, -1.0)
    local_id = idv - jc * cshard
    rank[1] = jnp.where(inside, (local_id // 256).astype(F32), 0.0)
    rank[2] = jnp.where(inside, lax.rem(local_id, 256).astype(F32), 0.0)
    want = lax.broadcasted_iota(jnp.int32, (256, 128), 0).astype(F32).astype(BF16)
    sub16 = lax.broadcasted_iota(jnp.int32, (16, 128), 0)
    lane16 = lax.broadcasted_iota(jnp.int32, (16, 128), 1)
    one_b, zero_b = jnp.ones((256, 128), BF16), jnp.zeros((256, 128), BF16)
    ssel[...] = jnp.zeros_like(ssel)

    def select(n, _):
        for v in range(4):
            q = n * 4 + v
            at = slice(v * 128, (v + 1) * 128)
            r = rank[0, pl.ds(q, 1), :]
            for u in range(share // 256):
                ru = jnp.broadcast_to((r - u * 256.0).astype(BF16), (256, 128))
                sel[u * 256:(u + 1) * 256, at] = jnp.where(want == ru, one_b, zero_b)
            place_hi = jnp.zeros((16, 128), jnp.int32) + (n * 2 + v // 2)
            place_lo = lane16 + (v % 2) * 128
            value = jnp.where(sub16 == 0, place_hi, place_lo).astype(F32)
            value = jnp.where(sub16 == 2, rank[1, pl.ds(q, 1), :], value)
            value = jnp.where(sub16 == 3, rank[2, pl.ds(q, 1), :], value)
            info[:, at] = value.astype(BF16)
        ssel[...] += dot(info[...], sel[...], NT)
        return 0

    lax.fori_loop(0, rows // 512, select, 0)
    lbuf[...] = (ssel[0:1, :] * 256.0 + ssel[1:2, :]).astype(jnp.int32)
    to_smem = pltpu.make_async_copy(lbuf, pick, lsem.at[13])
    to_smem.start()
    idbuf[...] = (ssel[2:3, :] * 256.0 + ssel[3:4, :]).astype(jnp.int32)
    rid[me] = idbuf[...]

    def id_copy(p, s):
        return pltpu.make_async_remote_copy(
            src_ref=idbuf, dst_ref=rid.at[s], send_sem=id_s.at[p], recv_sem=id_r.at[s],
            device_id={"dp": p}, device_id_type=MESH,
        )

    def ce_copy(p, s):
        return pltpu.make_async_remote_copy(
            src_ref=cs.at[p], dst_ref=rc.at[s], send_sem=ce_s.at[p], recv_sem=ce_r.at[s],
            device_id={"dp": p}, device_id_type=MESH,
        )

    to_smem.wait()

    def take(n, _):
        for u in range(16):
            p = n * 16 + u
            xc[pl.ds(pl.multiple_of(p * 8, 8), 8), :] = slabs[jnp.clip(pick[0, p], 0, rows - 1)]
        return 0

    lax.fori_loop(0, share // 16, take, 0)
    part = jnp.zeros((share, 128), F32)
    for c in range(8):
        v = xc[pl.ds(c, share, stride=8), :]
        part = part + v * v
    scale = 1.0 / jnp.sqrt(jnp.sum(part, axis=1, keepdims=True) + EPS)
    for c in range(8):
        v = (xc[pl.ds(c, share, stride=8), :] * scale).astype(BF16).T
        cs[2 * c] = v[:fpart]
        cs[2 * c + 1] = v[fpart:]
    rc[me] = cs[me]

    def send_cent(k, _):
        p = peer(k)
        id_copy(p, me).start()
        ce_copy(p, me).start()
        return 0

    lax.fori_loop(1, n_dp, send_cent, 0)

    def later_round(t, _):
        send_round(t)
        return 0

    lax.fori_loop(1, 4, later_round, 0)

    cent_load.wait()

    def unit_cent(n, _):
        r = pl.multiple_of(n * 128, 128)
        v = cen[pl.ds(r, 128), :].astype(F32)
        w = v * (1.0 / jnp.sqrt(jnp.sum(v * v, axis=1, keepdims=True) + EPS))
        cen[pl.ds(r, 128), :] = w.astype(BF16)
        return 0

    lax.fori_loop(0, cshard // 128, unit_cent, 0)

    def sq_copy(p, s):
        return pltpu.make_async_remote_copy(
            src_ref=ssq, dst_ref=rssq.at[s], send_sem=sq_s.at[p], recv_sem=sq_r.at[s],
            device_id={"dp": p}, device_id_type=MESH,
        )

    n_hi = cshard // lo_n
    want_lo = lax.broadcasted_iota(jnp.int32, (lo_n, share), 0).astype(F32).astype(BF16)
    one_s, zero_s = jnp.ones((lo_n, share), BF16), jnp.zeros((lo_n, share), BF16)
    zero_f = jnp.zeros((fpart, share), BF16)

    def place(s, u):
        ident = rid[s]
        low = (ident & (lo_n - 1)).astype(F32).astype(BF16)
        high = (ident // lo_n).astype(F32).astype(BF16)
        at = slice(u * share, (u + 1) * share)
        hot[:, at] = jnp.where(want_lo == jnp.broadcast_to(low, (lo_n, share)), one_s, zero_s)
        x = rc[s]
        hb = jnp.broadcast_to(high, (fpart, share))
        for h in range(n_hi):
            lhs[h * fpart:(h + 1) * fpart, at] = jnp.where(hb == float(h), x, zero_f)

    def arrived(k, _):
        s = peer(k)
        id_copy(s, s).wait_recv()
        ce_copy(s, s).wait_recv()
        return 0

    def add_group(g, _):
        for u in range(4):
            place(peer(g * 4 + u), u)
        acc[...] += dot(lhs[...], hot[...], NT)
        return 0

    def sum_rows():
        lax.fori_loop(1, n_dp, arrived, 0)
        acc[...] = jnp.zeros_like(acc)
        lax.fori_loop(0, 4, add_group, 0)
        for h in range(n_hi):
            a = acc[h * fpart:(h + 1) * fpart, :]
            ssq[h:h + 1, :] = jnp.sum(a * a, axis=0, keepdims=True)
        rssq[me] = ssq[...]

        def send_sq(k, _):
            sq_copy(peer(k), me).start()
            return 0

        lax.fori_loop(1, n_dp, send_sq, 0)

    blk = tmax.shape[0]

    def score(b, _):
        pl.when(b == rows // blk - 1)(sum_rows)
        r = pl.multiple_of(b * blk, blk)

        def tile(n, _):
            k0 = pl.multiple_of(n * blk, blk)
            s = dot(emb[pl.ds(r, blk), :], cen[pl.ds(k0, blk), :], NT)
            m = s[:, 0:128]
            for c in range(1, blk // 128):
                m = jnp.maximum(m, s[:, c * 128:(c + 1) * 128])
            tmax[...] = jnp.where(n == 0, m, jnp.maximum(tmax[...], m))
            return 0

        lax.fori_loop(0, cshard // blk, tile, 0)
        top = jnp.max(tmax[...].T, axis=0, keepdims=True)
        nrm = jnp.sqrt(jnp.sum(sqp[pl.ds(r, blk), :].T, axis=0, keepdims=True) + EPS)
        top = top / nrm
        for c in range(blk // 128):
            bloc[pl.ds(b * (blk // 128) + c, 1), :] = top[:, c * 128:(c + 1) * 128]
        return 0

    lax.fori_loop(0, rows // blk, score, 0)

    def be_copy(p, s):
        return pltpu.make_async_remote_copy(
            src_ref=bloc, dst_ref=rbest.at[s], send_sem=be_s.at[p], recv_sem=be_r.at[s],
            device_id={"cent": p}, device_id_type=MESH,
        )

    for k in range(1, n_cent):
        be_copy(cpeer(k), jc).start()

    pa = lax.broadcasted_iota(jnp.int32, (256, 256), 0)
    pb = lax.broadcasted_iota(jnp.int32, (256, 256), 1)
    diag = pa == pb

    def block(t, _):
        def arrive(k, _):
            s = peer(k)
            cl_copy(t, s, s).wait_recv()
            return 0

        lax.fori_loop(1, n_dp, arrive, 0)
        x = recv[t].reshape(256, feat)
        gm = dot(x, x, NT)
        dg = jnp.where(diag, gm, 0.0)
        icol = 1.0 / jnp.sqrt(jnp.sum(dg, axis=1, keepdims=True) + EPS)
        irow = 1.0 / jnp.sqrt(jnp.sum(dg, axis=0, keepdims=True) + EPS)
        v = gm * icol
        ok = (v == v) & jnp.logical_not(diag)
        m = jnp.max(jnp.where(ok, v, -jnp.inf), axis=0, keepdims=True)
        slot_out[pl.ds(t, 1), :] = jnp.where(m > -jnp.inf, m * irow, -1.0)
        return 0

    def got_sq(k, _):
        s = peer(k)
        sq_copy(s, s).wait_recv()
        return 0

    lax.fori_loop(1, n_dp, got_sq, 0)
    full = rssq[0]
    for s in range(1, n_dp):
        full = full + rssq[s]
    inv = 1.0 / jnp.maximum(jnp.sqrt(full), 1.0)
    for h in range(n_hi):
        new_out[:, h * lo_n:(h + 1) * lo_n] = (
            acc[h * fpart:(h + 1) * fpart, :] * inv[h:h + 1, :]
        )

    for k in range(1, n_cent):
        s = cpeer(k)
        be_copy(s, s).wait_recv()
    rbest[jc] = bloc[...]
    top = rbest[0]
    for s in range(1, n_cent):
        top = jnp.maximum(top, rbest[s])
    best_out[...] = top

    lax.fori_loop(0, 4, block, 0)

    def sent(k, _):
        p = peer(k)
        for t in range(4):
            cl_copy(t, p, me).wait_send()
        id_copy(p, me).wait_send()
        ce_copy(p, me).wait_send()
        sq_copy(p, me).wait_send()
        return 0

    lax.fori_loop(1, n_dp, sent, 0)
    for k in range(1, n_cent):
        be_copy(cpeer(k), jc).wait_send()


def hand_over(best, new, slot, best_out, new_out, slot_out):
    best_out[...] = best[...]
    new_out[...] = new[...]
    slot_out[...] = slot[...]


def shards(embeddings, centroids, kmeans_id, members, counts, owner_groups):
    rows, feat = embeddings.shape
    cshard = centroids.shape[0]
    vm = pl.BlockSpec(memory_space=pltpu.VMEM)
    hbm = pl.BlockSpec(memory_space=pltpu.MemorySpace.HBM)
    dma = pltpu.SemaphoreType.DMA
    tables = (
        owner_groups.transpose(1, 2, 0), members[:, 0, :].T,
        counts.reshape(-1), kmeans_id.reshape(32, 128),
    )
    best, new, slot = pl.pallas_call(
        body,
        out_shape=(
            jax.ShapeDtypeStruct((rows // 128, 128), F32),
            jax.ShapeDtypeStruct((feat // 16, cshard), F32),
            jax.ShapeDtypeStruct((4, 256), F32),
        ),
        in_specs=[hbm] * 6,
        out_specs=(vm, vm, vm),
        scratch_shapes=[
            pltpu.SMEM((8, 4, 16), jnp.int32),
            pltpu.SMEM((16, 512), jnp.int32),
            pltpu.SMEM((512,), jnp.int32),
            pltpu.VMEM((rows // 128, 128), jnp.int32),
            pltpu.SMEM((1, 512), jnp.int32),
            pltpu.VMEM((rows, feat), BF16),
            pltpu.VMEM((rows * 8 + 8, 128), F32),
            pltpu.VMEM((rows, 128), F32),
            pltpu.VMEM((cshard, feat), BF16),
            pltpu.VMEM((128, 128), F32),
            pltpu.VMEM((4, 16, 16, feat), BF16),
            pltpu.VMEM((4, 16, 16, feat), BF16),
            pltpu.VMEM((512 * 8, 128), F32),
            pltpu.VMEM((16, feat // 16, 512), BF16),
            pltpu.VMEM((16, feat // 16, 512), BF16),
            pltpu.VMEM((1, 512), jnp.int32),
            pltpu.VMEM((1, 512), jnp.int32),
            pltpu.VMEM((16, 1, 512), jnp.int32),
            pltpu.VMEM((3, 32, 128), F32),
            pltpu.VMEM((512, 512), BF16),
            pltpu.VMEM((16, 512), BF16),
            pltpu.VMEM((16, 512), F32),
            pltpu.VMEM((256, 2048), BF16),
            pltpu.VMEM((512, 2048), BF16),
            pltpu.VMEM((1024, 128), F32),
            pltpu.VMEM((rows // 128, 128), F32),
            pltpu.VMEM((8, rows // 128, 128), F32),
            pltpu.VMEM((512, 256), F32),
            pltpu.VMEM((8, 256), F32),
            pltpu.VMEM((16, 8, 256), F32),
            dma((14,)),
            dma((4, 16)), dma((4, 16)),
            dma((16,)), dma((16,)),
            dma((16,)), dma((16,)),
            dma((16,)), dma((16,)),
            dma((8,)), dma((8,)),
        ],
        compiler_params=pltpu.CompilerParams(
            collective_id=0, has_side_effects=True, vmem_limit_bytes=50 << 20
        ),
        name="window",
    )(
        *(pltpu.with_memory_space_constraint(v, pltpu.MemorySpace.HBM) for v in tables),
        embeddings,
        centroids,
    )
    best, new, slot = pl.pallas_call(
        hand_over,
        out_shape=tuple(jax.ShapeDtypeStruct(v.shape, v.dtype) for v in (best, new, slot)),
        in_specs=[vm, vm, vm],
        out_specs=(vm, vm, vm),
        compiler_params=pltpu.CompilerParams(vmem_limit_bytes=4 << 20),
        name="hand_over",
    )(best, new, slot)
    return best.reshape(rows), new, slot.reshape(1, 1, 4, 256)


def solution(mesh):
    placed = (P("dp", None), P("cent", None), P("dp"), P(None, "dp", None), P(None, "dp"), P())
    return jax.shard_map(
        shards,
        mesh=mesh,
        in_specs=placed,
        out_specs=(P("dp"), P("dp", "cent"), P("dp", "cent", None, None)),
        check_vma=False,
    )
```

```python
import functools

import jax
import jax.numpy as jnp
from jax import lax
from jax.experimental import pallas as pl
from jax.experimental.pallas import tpu as pltpu
from jax.sharding import PartitionSpec as P

EPS = 1e-06
MESH = pl.DeviceIdType.MESH
F32 = jnp.float32
BF16 = jnp.bfloat16
NT = (((1,), (1,)), ((), ()))
NN = (((1,), (0,)), ((), ()))


def dot(a, b, dims):
    return lax.dot_general(a, b, dims, preferred_element_type=F32)


def body(
    og_hbm, mem_hbm, cnt_hbm, ids_hbm, emb_hbm, cent_hbm,
    best_out, new_out, slot_out,
    og, mem, cnt, ids, pick, emb, x32, sqp, cen, g32, sb, recv, xc, cs, rc, idbuf, lbuf, rid, rank, sel, info, ssel, hot, lhs,
    tmax, bloc, rbest, acc, ssq, rssq,
    lsem, cl_s, cl_r, ce_s, ce_r, id_s, id_r, sq_s, sq_r, be_s, be_r,
):
    rows, feat = emb.shape
    n_dp, n_cent = 16, 8
    me = lax.axis_index("dp")
    jc = lax.axis_index("cent")
    mx, my = me // 4, lax.rem(me, 4)
    chunk = rows // 8
    share = pick.shape[1]
    cshard = cen.shape[0]
    lo_n = acc.shape[1]
    fpart = feat // n_dp

    def peer(k):
        return lax.rem(mx + k // 4, 4) * 4 + lax.rem(my + lax.rem(k, 4), 4)

    def cpeer(k):
        return lax.rem(jc + k, n_cent)

    slabs = x32.reshape(rows + 1, 8, 128)

    def load(i):
        return pltpu.make_async_copy(
            emb_hbm.at[pl.ds(i * chunk, chunk)], emb.at[pl.ds(i * chunk, chunk)], lsem.at[i]
        )

    cent_load = pltpu.make_async_copy(cent_hbm, cen, lsem.at[8])
    tables = [
        pltpu.make_async_copy(a, b, lsem.at[9 + i])
        for i, (a, b) in enumerate(((og_hbm, og), (mem_hbm, mem), (cnt_hbm, cnt), (ids_hbm, ids)))
    ]
    for c in tables:
        c.start()
    for i in range(8):
        load(i).start()

    barrier = pltpu.get_barrier_semaphore()
    for k in range(1, n_dp):
        pl.semaphore_signal(barrier, inc=1, device_id={"dp": peer(k)}, device_id_type=MESH)
    for k in range(1, n_cent):
        pl.semaphore_signal(barrier, inc=1, device_id={"cent": cpeer(k)}, device_id_type=MESH)

    x32[rows * 8:, :] = jnp.full((8, 128), jnp.nan, F32)

    def widen_chunk(i, _):
        load(i).wait()

        def widen(n, _):
            r = pl.multiple_of(i * chunk + n * 16, 16)
            square = jnp.zeros((16, 128), F32)
            for c in range(8):
                v = emb[pl.ds(r, 16), c * 128:(c + 1) * 128].astype(F32)
                x32[pl.ds(r * 8 + c, 16, stride=8), :] = v
                square = square + v * v
            sqp[pl.ds(r, 16), :] = square
            return 0

        lax.fori_loop(0, chunk // 16, widen, 0, unroll=4)
        return 0

    lax.fori_loop(0, 8, widen_chunk, 0)
    cent_load.start()
    for c in tables:
        c.wait()
    pl.semaphore_wait(barrier, n_dp + n_cent - 2)

    def gather(t, p, dst):
        g = og[jc, t, p]
        live = cnt[g]
        for q in range(16):
            row = jnp.where(q < live, mem[q, g], rows)
            g32[q * 8:(q + 1) * 8, :] = slabs[row]
        for c in range(8):
            dst[:, c * 128:(c + 1) * 128] = g32[pl.ds(c, 16, stride=8), :].astype(BF16)

    def cl_copy(t, p, s):
        return pltpu.make_async_remote_copy(
            src_ref=sb.at[t, p], dst_ref=recv.at[t, s],
            send_sem=cl_s.at[t, p], recv_sem=cl_r.at[t, s],
            device_id={"dp": p}, device_id_type=MESH,
        )

    def send_round(t):
        def step(k, _):
            p = peer(k)
            gather(t, p, sb.at[t, p])

            @pl.when(k > 0)
            def _():
                cl_copy(t, p, me).start()

            return 0

        lax.fori_loop(0, n_dp, step, 0, unroll=2)
        recv[t, me] = sb[t, me]

    send_round(0)

    idv = ids[...]
    inside = (idv // cshard) == jc
    insf = inside.astype(F32).astype(BF16)
    lane_a = lax.broadcasted_iota(jnp.int32, (128, 128), 0)
    lane_b = lax.broadcasted_iota(jnp.int32, (128, 128), 1)
    upper = (lane_a <= lane_b).astype(F32).astype(BF16)
    run = dot(insf, upper, NN)
    total = dot(insf, jnp.ones((128, 128), BF16), NN).astype(BF16)
    row_a = lax.broadcasted_iota(jnp.int32, (32, 32), 0)
    row_b = lax.broadcasted_iota(jnp.int32, (32, 32), 1)
    lower = (row_b < row_a).astype(F32).astype(BF16)
    before = dot(lower, total, NN)
    rank[0] = jnp.where(inside, before + run - 1.0, -1.0)
    local_id = idv - jc * cshard
    rank[1] = jnp.where(inside, (local_id // 256).astype(F32), 0.0)
    rank[2] = jnp.where(inside, lax.rem(local_id, 256).astype(F32), 0.0)
    want = lax.broadcasted_iota(jnp.int32, (256, 128), 0).astype(F32).astype(BF16)
    sub16 = lax.broadcasted_iota(jnp.int32, (16, 128), 0)
    lane16 = lax.broadcasted_iota(jnp.int32, (16, 128), 1)
    one_b, zero_b = jnp.ones((256, 128), BF16), jnp.zeros((256, 128), BF16)
    ssel[...] = jnp.zeros_like(ssel)

    def select(n, _):
        for v in range(4):
            q = n * 4 + v
            at = slice(v * 128, (v + 1) * 128)
            r = rank[0, pl.ds(q, 1), :]
            for u in range(share // 256):
                ru = jnp.broadcast_to((r - u * 256.0).astype(BF16), (256, 128))
                sel[u * 256:(u + 1) * 256, at] = jnp.where(want == ru, one_b, zero_b)
            place_hi = jnp.zeros((16, 128), jnp.int32) + (n * 2 + v // 2)
            place_lo = lane16 + (v % 2) * 128
            value = jnp.where(sub16 == 0, place_hi, place_lo).astype(F32)
            value = jnp.where(sub16 == 2, rank[1, pl.ds(q, 1), :], value)
            value = jnp.where(sub16 == 3, rank[2, pl.ds(q, 1), :], value)
            info[:, at] = value.astype(BF16)
        ssel[...] += dot(info[...], sel[...], NT)
        return 0

    lax.fori_loop(0, rows // 512, select, 0)
    lbuf[...] = (ssel[0:1, :] * 256.0 + ssel[1:2, :]).astype(jnp.int32)
    to_smem = pltpu.make_async_copy(lbuf, pick, lsem.at[13])
    to_smem.start()
    idbuf[...] = (ssel[2:3, :] * 256.0 + ssel[3:4, :]).astype(jnp.int32)
    rid[me] = idbuf[...]

    def id_copy(p, s):
        return pltpu.make_async_remote_copy(
            src_ref=idbuf, dst_ref=rid.at[s], send_sem=id_s.at[p], recv_sem=id_r.at[s],
            device_id={"dp": p}, device_id_type=MESH,
        )

    def ce_copy(p, s):
        return pltpu.make_async_remote_copy(
            src_ref=cs.at[p], dst_ref=rc.at[s], send_sem=ce_s.at[p], recv_sem=ce_r.at[s],
            device_id={"dp": p}, device_id_type=MESH,
        )

    to_smem.wait()

    def take(n, _):
        for u in range(16):
            p = n * 16 + u
            xc[pl.ds(pl.multiple_of(p * 8, 8), 8), :] = slabs[jnp.clip(pick[0, p], 0, rows - 1)]
        return 0

    lax.fori_loop(0, share // 16, take, 0)
    part = jnp.zeros((share, 128), F32)
    for c in range(8):
        v = xc[pl.ds(c, share, stride=8), :]
        part = part + v * v
    scale = 1.0 / jnp.sqrt(jnp.sum(part, axis=1, keepdims=True) + EPS)
    for c in range(8):
        v = (xc[pl.ds(c, share, stride=8), :] * scale).astype(BF16).T
        cs[2 * c] = v[:fpart]
        cs[2 * c + 1] = v[fpart:]
    rc[me] = cs[me]

    def send_cent(k, _):
        p = peer(k)
        id_copy(p, me).start()
        ce_copy(p, me).start()
        return 0

    lax.fori_loop(1, n_dp, send_cent, 0)

    def later_round(t, _):
        send_round(t)
        return 0

    lax.fori_loop(1, 4, later_round, 0)

    cent_load.wait()

    def unit_cent(n, _):
        r = pl.multiple_of(n * 128, 128)
        v = cen[pl.ds(r, 128), :].astype(F32)
        w = v * (1.0 / jnp.sqrt(jnp.sum(v * v, axis=1, keepdims=True) + EPS))
        cen[pl.ds(r, 128), :] = w.astype(BF16)
        return 0

    lax.fori_loop(0, cshard // 128, unit_cent, 0)

    def sq_copy(p, s):
        return pltpu.make_async_remote_copy(
            src_ref=ssq, dst_ref=rssq.at[s], send_sem=sq_s.at[p], recv_sem=sq_r.at[s],
            device_id={"dp": p}, device_id_type=MESH,
        )

    n_hi = cshard // lo_n
    want_lo = lax.broadcasted_iota(jnp.int32, (lo_n, share), 0).astype(F32).astype(BF16)
    one_s, zero_s = jnp.ones((lo_n, share), BF16), jnp.zeros((lo_n, share), BF16)
    zero_f = jnp.zeros((fpart, share), BF16)

    def place(s, u):
        ident = rid[s]
        low = (ident & (lo_n - 1)).astype(F32).astype(BF16)
        high = (ident // lo_n).astype(F32).astype(BF16)
        at = slice(u * share, (u + 1) * share)
        hot[:, at] = jnp.where(want_lo == jnp.broadcast_to(low, (lo_n, share)), one_s, zero_s)
        x = rc[s]
        hb = jnp.broadcast_to(high, (fpart, share))
        for h in range(n_hi):
            lhs[h * fpart:(h + 1) * fpart, at] = jnp.where(hb == float(h), x, zero_f)

    def arrived(k, _):
        s = peer(k)
        id_copy(s, s).wait_recv()
        ce_copy(s, s).wait_recv()
        return 0

    def add_group(g, _):
        for u in range(4):
            place(peer(g * 4 + u), u)
        acc[...] += dot(lhs[...], hot[...], NT)
        return 0

    def sum_rows():
        lax.fori_loop(1, n_dp, arrived, 0)
        acc[...] = jnp.zeros_like(acc)
        lax.fori_loop(0, 4, add_group, 0)
        for h in range(n_hi):
            a = acc[h * fpart:(h + 1) * fpart, :]
            ssq[h:h + 1, :] = jnp.sum(a * a, axis=0, keepdims=True)
        rssq[me] = ssq[...]

        def send_sq(k, _):
            sq_copy(peer(k), me).start()
            return 0

        lax.fori_loop(1, n_dp, send_sq, 0)

    blk = tmax.shape[0]

    def score(b, _):
        pl.when(b == rows // blk - 1)(sum_rows)
        r = pl.multiple_of(b * blk, blk)

        def tile(n, _):
            k0 = pl.multiple_of(n * blk, blk)
            s = dot(emb[pl.ds(r, blk), :], cen[pl.ds(k0, blk), :], NT)
            m = s[:, 0:128]
            for c in range(1, blk // 128):
                m = jnp.maximum(m, s[:, c * 128:(c + 1) * 128])
            tmax[...] = jnp.where(n == 0, m, jnp.maximum(tmax[...], m))
            return 0

        lax.fori_loop(0, cshard // blk, tile, 0)
        top = jnp.max(tmax[...].T, axis=0, keepdims=True)
        nrm = jnp.sqrt(jnp.sum(sqp[pl.ds(r, blk), :].T, axis=0, keepdims=True) + EPS)
        top = top / nrm
        for c in range(blk // 128):
            bloc[pl.ds(b * (blk // 128) + c, 1), :] = top[:, c * 128:(c + 1) * 128]
        return 0

    lax.fori_loop(0, rows // blk, score, 0)

    def be_copy(p, s):
        return pltpu.make_async_remote_copy(
            src_ref=bloc, dst_ref=rbest.at[s], send_sem=be_s.at[p], recv_sem=be_r.at[s],
            device_id={"cent": p}, device_id_type=MESH,
        )

    for k in range(1, n_cent):
        be_copy(cpeer(k), jc).start()

    pa = lax.broadcasted_iota(jnp.int32, (256, 256), 0)
    pb = lax.broadcasted_iota(jnp.int32, (256, 256), 1)
    diag = pa == pb

    def block(t, _):
        def arrive(k, _):
            s = peer(k)
            cl_copy(t, s, s).wait_recv()
            return 0

        lax.fori_loop(1, n_dp, arrive, 0)
        x = recv[t].reshape(256, feat)
        gm = dot(x, x, NT)
        dg = jnp.where(diag, gm, 0.0)
        icol = 1.0 / jnp.sqrt(jnp.sum(dg, axis=1, keepdims=True) + EPS)
        irow = 1.0 / jnp.sqrt(jnp.sum(dg, axis=0, keepdims=True) + EPS)
        v = gm * icol
        ok = (v == v) & jnp.logical_not(diag)
        m = jnp.max(jnp.where(ok, v, -jnp.inf), axis=0, keepdims=True)
        slot_out[pl.ds(t, 1), :] = jnp.where(m > -jnp.inf, m * irow, -1.0)
        return 0

    lax.fori_loop(0, 4, block, 0)

    def got_sq(k, _):
        s = peer(k)
        sq_copy(s, s).wait_recv()
        return 0

    lax.fori_loop(1, n_dp, got_sq, 0)
    full = rssq[0]
    for s in range(1, n_dp):
        full = full + rssq[s]
    inv = 1.0 / jnp.maximum(jnp.sqrt(full), 1.0)
    for h in range(n_hi):
        new_out[:, h * lo_n:(h + 1) * lo_n] = (
            acc[h * fpart:(h + 1) * fpart, :] * inv[h:h + 1, :]
        )

    for k in range(1, n_cent):
        s = cpeer(k)
        be_copy(s, s).wait_recv()
    rbest[jc] = bloc[...]
    top = rbest[0]
    for s in range(1, n_cent):
        top = jnp.maximum(top, rbest[s])
    best_out[...] = top


    def sent(k, _):
        p = peer(k)
        for t in range(4):
            cl_copy(t, p, me).wait_send()
        id_copy(p, me).wait_send()
        ce_copy(p, me).wait_send()
        sq_copy(p, me).wait_send()
        return 0

    lax.fori_loop(1, n_dp, sent, 0)
    for k in range(1, n_cent):
        be_copy(cpeer(k), jc).wait_send()


def hand_over(best, new, slot, best_out, new_out, slot_out):
    best_out[...] = best[...]
    new_out[...] = new[...]
    slot_out[...] = slot[...]


def shards(embeddings, centroids, kmeans_id, members, counts, owner_groups):
    rows, feat = embeddings.shape
    cshard = centroids.shape[0]
    vm = pl.BlockSpec(memory_space=pltpu.VMEM)
    hbm = pl.BlockSpec(memory_space=pltpu.MemorySpace.HBM)
    dma = pltpu.SemaphoreType.DMA
    tables = (
        owner_groups.transpose(1, 2, 0), members[:, 0, :].T,
        counts.reshape(-1), kmeans_id.reshape(32, 128),
    )
    best, new, slot = pl.pallas_call(
        body,
        out_shape=(
            jax.ShapeDtypeStruct((rows // 128, 128), F32),
            jax.ShapeDtypeStruct((feat // 16, cshard), F32),
            jax.ShapeDtypeStruct((4, 256), F32),
        ),
        in_specs=[hbm] * 6,
        out_specs=(vm, vm, vm),
        scratch_shapes=[
            pltpu.SMEM((8, 4, 16), jnp.int32),
            pltpu.SMEM((16, 512), jnp.int32),
            pltpu.SMEM((512,), jnp.int32),
            pltpu.VMEM((rows // 128, 128), jnp.int32),
            pltpu.SMEM((1, 512), jnp.int32),
            pltpu.VMEM((rows, feat), BF16),
            pltpu.VMEM((rows * 8 + 8, 128), F32),
            pltpu.VMEM((rows, 128), F32),
            pltpu.VMEM((cshard, feat), BF16),
            pltpu.VMEM((128, 128), F32),
            pltpu.VMEM((4, 16, 16, feat), BF16),
            pltpu.VMEM((4, 16, 16, feat), BF16),
            pltpu.VMEM((512 * 8, 128), F32),
            pltpu.VMEM((16, feat // 16, 512), BF16),
            pltpu.VMEM((16, feat // 16, 512), BF16),
            pltpu.VMEM((1, 512), jnp.int32),
            pltpu.VMEM((1, 512), jnp.int32),
            pltpu.VMEM((16, 1, 512), jnp.int32),
            pltpu.VMEM((3, 32, 128), F32),
            pltpu.VMEM((512, 512), BF16),
            pltpu.VMEM((16, 512), BF16),
            pltpu.VMEM((16, 512), F32),
            pltpu.VMEM((256, 2048), BF16),
            pltpu.VMEM((512, 2048), BF16),
            pltpu.VMEM((1024, 128), F32),
            pltpu.VMEM((rows // 128, 128), F32),
            pltpu.VMEM((8, rows // 128, 128), F32),
            pltpu.VMEM((512, 256), F32),
            pltpu.VMEM((8, 256), F32),
            pltpu.VMEM((16, 8, 256), F32),
            dma((14,)),
            dma((4, 16)), dma((4, 16)),
            dma((16,)), dma((16,)),
            dma((16,)), dma((16,)),
            dma((16,)), dma((16,)),
            dma((8,)), dma((8,)),
        ],
        compiler_params=pltpu.CompilerParams(
            collective_id=0, has_side_effects=True, vmem_limit_bytes=50 << 20
        ),
        name="window",
    )(
        *(pltpu.with_memory_space_constraint(v, pltpu.MemorySpace.HBM) for v in tables),
        embeddings,
        centroids,
    )
    best, new, slot = pl.pallas_call(
        hand_over,
        out_shape=tuple(jax.ShapeDtypeStruct(v.shape, v.dtype) for v in (best, new, slot)),
        in_specs=[vm, vm, vm],
        out_specs=(vm, vm, vm),
        compiler_params=pltpu.CompilerParams(vmem_limit_bytes=4 << 20),
        name="hand_over",
    )(best, new, slot)
    return best.reshape(rows), new, slot.reshape(1, 1, 4, 256)


def solution(mesh):
    placed = (P("dp", None), P("cent", None), P("dp"), P(None, "dp", None), P(None, "dp"), P())
    return jax.shard_map(
        shards,
        mesh=mesh,
        in_specs=placed,
        out_specs=(P("dp"), P("dp", "cent"), P("dp", "cent", None, None)),
        check_vma=False,
    )
```

```python
import functools

import jax
import jax.numpy as jnp
from jax import lax
from jax.experimental import pallas as pl
from jax.experimental.pallas import tpu as pltpu
from jax.sharding import PartitionSpec as P

EPS = 1e-06
MESH = pl.DeviceIdType.MESH
F32 = jnp.float32
BF16 = jnp.bfloat16
NT = (((1,), (1,)), ((), ()))
NN = (((1,), (0,)), ((), ()))


def dot(a, b, dims):
    return lax.dot_general(a, b, dims, preferred_element_type=F32)


def body(
    og_hbm, mem_hbm, cnt_hbm, ids_hbm, emb_hbm, cent_hbm,
    best_out, new_out, slot_out,
    og, mem, cnt, ids, pick, emb, x32, sqp, cen, g32, sb, recv, xc, cs, rc, idbuf, lbuf, rid, rank, sel, info, ssel, hot, lhs,
    tmax, bloc, rbest, acc, ssq, rssq,
    lsem, cl_s, cl_r, ce_s, ce_r, id_s, id_r, sq_s, sq_r, be_s, be_r,
):
    rows, feat = emb.shape
    n_dp, n_cent = 16, 8
    me = lax.axis_index("dp")
    jc = lax.axis_index("cent")
    mx, my = me // 4, lax.rem(me, 4)
    chunk = rows // 4
    share = pick.shape[1]
    cshard = cen.shape[0]
    lo_n = acc.shape[1]
    fpart = feat // n_dp

    def peer(i):
        k = lax.rem(i * 7, 16)
        return lax.rem(mx + k // 4, 4) * 4 + lax.rem(my + lax.rem(k, 4), 4)

    def cpeer(k):
        return lax.rem(jc + k, n_cent)

    slabs = x32.reshape(rows + 1, 8, 128)

    def load(i):
        return pltpu.make_async_copy(
            emb_hbm.at[pl.ds(i * chunk, chunk)], emb.at[pl.ds(i * chunk, chunk)], lsem.at[i]
        )

    cent_load = pltpu.make_async_copy(cent_hbm, cen, lsem.at[8])
    tables = [
        pltpu.make_async_copy(a, b, lsem.at[9 + i])
        for i, (a, b) in enumerate(((og_hbm, og), (mem_hbm, mem), (cnt_hbm, cnt), (ids_hbm, ids)))
    ]
    for c in tables:
        c.start()
    for i in range(4):
        load(i).start()

    barrier = pltpu.get_barrier_semaphore()
    for k in range(1, n_dp):
        pl.semaphore_signal(barrier, inc=1, device_id={"dp": peer(k)}, device_id_type=MESH)
    for k in range(1, n_cent):
        pl.semaphore_signal(barrier, inc=1, device_id={"cent": cpeer(k)}, device_id_type=MESH)

    x32[rows * 8:, :] = jnp.full((8, 128), jnp.nan, F32)

    def widen_chunk(i, _):
        load(i).wait()

        def widen(n, _):
            r = pl.multiple_of(i * chunk + n * 16, 16)
            square = jnp.zeros((16, 128), F32)
            for c in range(8):
                v = emb[pl.ds(r, 16), c * 128:(c + 1) * 128].astype(F32)
                x32[pl.ds(r * 8 + c, 16, stride=8), :] = v
                square = square + v * v
            sqp[pl.ds(r, 16), :] = square
            return 0

        lax.fori_loop(0, chunk // 16, widen, 0, unroll=4)
        return 0

    lax.fori_loop(0, 4, widen_chunk, 0)
    cent_load.start()
    for c in tables:
        c.wait()
    pl.semaphore_wait(barrier, n_dp + n_cent - 2)

    def gather(t, p, dst):
        g = og[jc, t, p]
        live = cnt[g]
        for q in range(16):
            row = jnp.where(q < live, mem[q, g], rows)
            g32[q * 8:(q + 1) * 8, :] = slabs[row]
        for c in range(8):
            dst[:, c * 128:(c + 1) * 128] = g32[pl.ds(c, 16, stride=8), :].astype(BF16)

    def cl_copy(t, p, s):
        return pltpu.make_async_remote_copy(
            src_ref=sb.at[t, p], dst_ref=recv.at[t, s],
            send_sem=cl_s.at[t, p], recv_sem=cl_r.at[t, s],
            device_id={"dp": p}, device_id_type=MESH,
        )

    def send_round(t):
        def step(k, _):
            p = peer(k)
            gather(t, p, sb.at[t, p])

            @pl.when(k > 0)
            def _():
                cl_copy(t, p, me).start()

            return 0

        lax.fori_loop(0, n_dp, step, 0, unroll=2)
        recv[t, me] = sb[t, me]

    send_round(0)

    idv = ids[...]
    inside = (idv // cshard) == jc
    insf = inside.astype(F32).astype(BF16)
    lane_a = lax.broadcasted_iota(jnp.int32, (128, 128), 0)
    lane_b = lax.broadcasted_iota(jnp.int32, (128, 128), 1)
    upper = (lane_a <= lane_b).astype(F32).astype(BF16)
    run = dot(insf, upper, NN)
    total = dot(insf, jnp.ones((128, 128), BF16), NN).astype(BF16)
    row_a = lax.broadcasted_iota(jnp.int32, (32, 32), 0)
    row_b = lax.broadcasted_iota(jnp.int32, (32, 32), 1)
    lower = (row_b < row_a).astype(F32).astype(BF16)
    before = dot(lower, total, NN)
    rank[0] = jnp.where(inside, before + run - 1.0, -1.0)
    local_id = idv - jc * cshard
    rank[1] = jnp.where(inside, (local_id // 256).astype(F32), 0.0)
    rank[2] = jnp.where(inside, lax.rem(local_id, 256).astype(F32), 0.0)
    want = lax.broadcasted_iota(jnp.int32, (256, 128), 0).astype(F32).astype(BF16)
    sub16 = lax.broadcasted_iota(jnp.int32, (16, 128), 0)
    lane16 = lax.broadcasted_iota(jnp.int32, (16, 128), 1)
    one_b, zero_b = jnp.ones((256, 128), BF16), jnp.zeros((256, 128), BF16)
    ssel[...] = jnp.zeros_like(ssel)

    def select(n, _):
        for v in range(4):
            q = n * 4 + v
            at = slice(v * 128, (v + 1) * 128)
            r = rank[0, pl.ds(q, 1), :]
            for u in range(share // 256):
                ru = jnp.broadcast_to((r - u * 256.0).astype(BF16), (256, 128))
                sel[u * 256:(u + 1) * 256, at] = jnp.where(want == ru, one_b, zero_b)
            place_hi = jnp.zeros((16, 128), jnp.int32) + (n * 2 + v // 2)
            place_lo = lane16 + (v % 2) * 128
            value = jnp.where(sub16 == 0, place_hi, place_lo).astype(F32)
            value = jnp.where(sub16 == 2, rank[1, pl.ds(q, 1), :], value)
            value = jnp.where(sub16 == 3, rank[2, pl.ds(q, 1), :], value)
            info[:, at] = value.astype(BF16)
        ssel[...] += dot(info[...], sel[...], NT)
        return 0

    lax.fori_loop(0, rows // 512, select, 0)
    lbuf[...] = (ssel[0:1, :] * 256.0 + ssel[1:2, :]).astype(jnp.int32)
    to_smem = pltpu.make_async_copy(lbuf, pick, lsem.at[13])
    to_smem.start()
    idbuf[...] = (ssel[2:3, :] * 256.0 + ssel[3:4, :]).astype(jnp.int32)
    rid[me] = idbuf[...]

    def id_copy(p, s):
        return pltpu.make_async_remote_copy(
            src_ref=idbuf, dst_ref=rid.at[s], send_sem=id_s.at[p], recv_sem=id_r.at[s],
            device_id={"dp": p}, device_id_type=MESH,
        )

    def ce_copy(p, s):
        return pltpu.make_async_remote_copy(
            src_ref=cs.at[p], dst_ref=rc.at[s], send_sem=ce_s.at[p], recv_sem=ce_r.at[s],
            device_id={"dp": p}, device_id_type=MESH,
        )

    to_smem.wait()

    def take(n, _):
        for u in range(16):
            p = n * 16 + u
            xc[pl.ds(pl.multiple_of(p * 8, 8), 8), :] = slabs[jnp.clip(pick[0, p], 0, rows - 1)]
        return 0

    lax.fori_loop(0, share // 16, take, 0)
    part = jnp.zeros((share, 128), F32)
    for c in range(8):
        v = xc[pl.ds(c, share, stride=8), :]
        part = part + v * v
    scale = 1.0 / jnp.sqrt(jnp.sum(part, axis=1, keepdims=True) + EPS)
    for c in range(8):
        v = (xc[pl.ds(c, share, stride=8), :] * scale).astype(BF16).T
        cs[2 * c] = v[:fpart]
        cs[2 * c + 1] = v[fpart:]
    rc[me] = cs[me]

    def send_cent(k, _):
        p = peer(k)
        id_copy(p, me).start()
        ce_copy(p, me).start()
        return 0

    lax.fori_loop(1, n_dp, send_cent, 0)

    def later_round(t, _):
        send_round(t)
        return 0

    lax.fori_loop(1, 4, later_round, 0)

    cent_load.wait()

    def unit_cent(n, _):
        r = pl.multiple_of(n * 128, 128)
        v = cen[pl.ds(r, 128), :].astype(F32)
        w = v * (1.0 / jnp.sqrt(jnp.sum(v * v, axis=1, keepdims=True) + EPS))
        cen[pl.ds(r, 128), :] = w.astype(BF16)
        return 0

    lax.fori_loop(0, cshard // 128, unit_cent, 0)

    def sq_copy(p, s):
        return pltpu.make_async_remote_copy(
            src_ref=ssq, dst_ref=rssq.at[s], send_sem=sq_s.at[p], recv_sem=sq_r.at[s],
            device_id={"dp": p}, device_id_type=MESH,
        )

    n_hi = cshard // lo_n
    want_lo = lax.broadcasted_iota(jnp.int32, (lo_n, share), 0).astype(F32).astype(BF16)
    one_s, zero_s = jnp.ones((lo_n, share), BF16), jnp.zeros((lo_n, share), BF16)
    zero_f = jnp.zeros((fpart, share), BF16)

    def place(s, u):
        ident = rid[s]
        low = (ident & (lo_n - 1)).astype(F32).astype(BF16)
        high = (ident // lo_n).astype(F32).astype(BF16)
        at = slice(u * share, (u + 1) * share)
        hot[:, at] = jnp.where(want_lo == jnp.broadcast_to(low, (lo_n, share)), one_s, zero_s)
        x = rc[s]
        hb = jnp.broadcast_to(high, (fpart, share))
        for h in range(n_hi):
            lhs[h * fpart:(h + 1) * fpart, at] = jnp.where(hb == float(h), x, zero_f)

    def arrived(k, _):
        s = peer(k)
        id_copy(s, s).wait_recv()
        ce_copy(s, s).wait_recv()
        return 0

    def add_group(g, _):
        for u in range(4):
            place(peer(g * 4 + u), u)
        acc[...] += dot(lhs[...], hot[...], NT)
        return 0

    def sum_rows():
        lax.fori_loop(1, n_dp, arrived, 0)
        acc[...] = jnp.zeros_like(acc)
        lax.fori_loop(0, 4, add_group, 0)
        for h in range(n_hi):
            a = acc[h * fpart:(h + 1) * fpart, :]
            ssq[h:h + 1, :] = jnp.sum(a * a, axis=0, keepdims=True)
        rssq[me] = ssq[...]

        def send_sq(k, _):
            sq_copy(peer(k), me).start()
            return 0

        lax.fori_loop(1, n_dp, send_sq, 0)

    blk = tmax.shape[0]

    def score(b, _):
        pl.when(b == rows // blk - 1)(sum_rows)
        r = pl.multiple_of(b * blk, blk)

        def tile(n, _):
            k0 = pl.multiple_of(n * blk, blk)
            s = dot(emb[pl.ds(r, blk), :], cen[pl.ds(k0, blk), :], NT)
            m = s[:, 0:128]
            for c in range(1, blk // 128):
                m = jnp.maximum(m, s[:, c * 128:(c + 1) * 128])
            tmax[...] = jnp.where(n == 0, m, jnp.maximum(tmax[...], m))
            return 0

        lax.fori_loop(0, cshard // blk, tile, 0)
        top = jnp.max(tmax[...].T, axis=0, keepdims=True)
        nrm = jnp.sqrt(jnp.sum(sqp[pl.ds(r, blk), :].T, axis=0, keepdims=True) + EPS)
        top = top / nrm
        for c in range(blk // 128):
            bloc[pl.ds(b * (blk // 128) + c, 1), :] = top[:, c * 128:(c + 1) * 128]
        return 0

    lax.fori_loop(0, rows // blk, score, 0)

    def be_copy(p, s):
        return pltpu.make_async_remote_copy(
            src_ref=bloc, dst_ref=rbest.at[s], send_sem=be_s.at[p], recv_sem=be_r.at[s],
            device_id={"cent": p}, device_id_type=MESH,
        )

    for k in range(1, n_cent):
        be_copy(cpeer(k), jc).start()

    pa = lax.broadcasted_iota(jnp.int32, (256, 256), 0)
    pb = lax.broadcasted_iota(jnp.int32, (256, 256), 1)
    diag = pa == pb

    def block(t, _):
        def arrive(k, _):
            s = peer(k)
            cl_copy(t, s, s).wait_recv()
            return 0

        lax.fori_loop(1, n_dp, arrive, 0)
        x = recv[t].reshape(256, feat)
        gm = dot(x, x, NT)
        dg = jnp.where(diag, gm, 0.0)
        icol = 1.0 / jnp.sqrt(jnp.sum(dg, axis=1, keepdims=True) + EPS)
        irow = 1.0 / jnp.sqrt(jnp.sum(dg, axis=0, keepdims=True) + EPS)
        v = gm * icol
        ok = (v == v) & jnp.logical_not(diag)
        m = jnp.max(jnp.where(ok, v, -jnp.inf), axis=0, keepdims=True)
        slot_out[pl.ds(t, 1), :] = jnp.where(m > -jnp.inf, m * irow, -1.0)
        return 0

    lax.fori_loop(0, 4, block, 0)

    def got_sq(k, _):
        s = peer(k)
        sq_copy(s, s).wait_recv()
        return 0

    lax.fori_loop(1, n_dp, got_sq, 0)
    full = rssq[0]
    for s in range(1, n_dp):
        full = full + rssq[s]
    inv = 1.0 / jnp.maximum(jnp.sqrt(full), 1.0)
    for h in range(n_hi):
        new_out[:, h * lo_n:(h + 1) * lo_n] = (
            acc[h * fpart:(h + 1) * fpart, :] * inv[h:h + 1, :]
        )

    for k in range(1, n_cent):
        s = cpeer(k)
        be_copy(s, s).wait_recv()
    rbest[jc] = bloc[...]
    top = rbest[0]
    for s in range(1, n_cent):
        top = jnp.maximum(top, rbest[s])
    best_out[...] = top


    def sent(k, _):
        p = peer(k)
        for t in range(4):
            cl_copy(t, p, me).wait_send()
        id_copy(p, me).wait_send()
        ce_copy(p, me).wait_send()
        sq_copy(p, me).wait_send()
        return 0

    lax.fori_loop(1, n_dp, sent, 0)
    for k in range(1, n_cent):
        be_copy(cpeer(k), jc).wait_send()


def hand_over(best, new, slot, best_out, new_out, slot_out):
    best_out[...] = best[...]
    new_out[...] = new[...]
    slot_out[...] = slot[...]


def shards(embeddings, centroids, kmeans_id, members, counts, owner_groups):
    rows, feat = embeddings.shape
    cshard = centroids.shape[0]
    vm = pl.BlockSpec(memory_space=pltpu.VMEM)
    hbm = pl.BlockSpec(memory_space=pltpu.MemorySpace.HBM)
    dma = pltpu.SemaphoreType.DMA
    tables = (
        owner_groups.transpose(1, 2, 0), members[:, 0, :].T,
        counts.reshape(-1), kmeans_id.reshape(32, 128),
    )
    best, new, slot = pl.pallas_call(
        body,
        out_shape=(
            jax.ShapeDtypeStruct((rows // 128, 128), F32),
            jax.ShapeDtypeStruct((feat // 16, cshard), F32),
            jax.ShapeDtypeStruct((4, 256), F32),
        ),
        in_specs=[hbm] * 6,
        out_specs=(vm, vm, vm),
        scratch_shapes=[
            pltpu.SMEM((8, 4, 16), jnp.int32),
            pltpu.SMEM((16, 512), jnp.int32),
            pltpu.SMEM((512,), jnp.int32),
            pltpu.VMEM((rows // 128, 128), jnp.int32),
            pltpu.SMEM((1, 512), jnp.int32),
            pltpu.VMEM((rows, feat), BF16),
            pltpu.VMEM((rows * 8 + 8, 128), F32),
            pltpu.VMEM((rows, 128), F32),
            pltpu.VMEM((cshard, feat), BF16),
            pltpu.VMEM((128, 128), F32),
            pltpu.VMEM((4, 16, 16, feat), BF16),
            pltpu.VMEM((4, 16, 16, feat), BF16),
            pltpu.VMEM((512 * 8, 128), F32),
            pltpu.VMEM((16, feat // 16, 512), BF16),
            pltpu.VMEM((16, feat // 16, 512), BF16),
            pltpu.VMEM((1, 512), jnp.int32),
            pltpu.VMEM((1, 512), jnp.int32),
            pltpu.VMEM((16, 1, 512), jnp.int32),
            pltpu.VMEM((3, 32, 128), F32),
            pltpu.VMEM((512, 512), BF16),
            pltpu.VMEM((16, 512), BF16),
            pltpu.VMEM((16, 512), F32),
            pltpu.VMEM((256, 2048), BF16),
            pltpu.VMEM((512, 2048), BF16),
            pltpu.VMEM((1024, 128), F32),
            pltpu.VMEM((rows // 128, 128), F32),
            pltpu.VMEM((8, rows // 128, 128), F32),
            pltpu.VMEM((512, 256), F32),
            pltpu.VMEM((8, 256), F32),
            pltpu.VMEM((16, 8, 256), F32),
            dma((14,)),
            dma((4, 16)), dma((4, 16)),
            dma((16,)), dma((16,)),
            dma((16,)), dma((16,)),
            dma((16,)), dma((16,)),
            dma((8,)), dma((8,)),
        ],
        compiler_params=pltpu.CompilerParams(
            collective_id=0, has_side_effects=True, vmem_limit_bytes=50 << 20
        ),
        name="window",
    )(
        *(pltpu.with_memory_space_constraint(v, pltpu.MemorySpace.HBM) for v in tables),
        embeddings,
        centroids,
    )
    best, new, slot = pl.pallas_call(
        hand_over,
        out_shape=tuple(jax.ShapeDtypeStruct(v.shape, v.dtype) for v in (best, new, slot)),
        in_specs=[vm, vm, vm],
        out_specs=(vm, vm, vm),
        compiler_params=pltpu.CompilerParams(vmem_limit_bytes=4 << 20),
        name="hand_over",
    )(best, new, slot)
    return best.reshape(rows), new, slot.reshape(1, 1, 4, 256)


def solution(mesh):
    placed = (P("dp", None), P("cent", None), P("dp"), P(None, "dp", None), P(None, "dp"), P())
    return jax.shard_map(
        shards,
        mesh=mesh,
        in_specs=placed,
        out_specs=(P("dp"), P("dp", "cent"), P("dp", "cent", None, None)),
        check_vma=False,
    )
```

```python
import functools

import jax
import jax.numpy as jnp
from jax import lax
from jax.experimental import pallas as pl
from jax.experimental.pallas import tpu as pltpu
from jax.sharding import PartitionSpec as P

EPS = 1e-06
MESH = pl.DeviceIdType.MESH
F32 = jnp.float32
BF16 = jnp.bfloat16
NT = (((1,), (1,)), ((), ()))
NN = (((1,), (0,)), ((), ()))


def dot(a, b, dims):
    return lax.dot_general(a, b, dims, preferred_element_type=F32)


def body(
    og_hbm, mem_hbm, cnt_hbm, ids_hbm, emb_hbm, cent_hbm,
    best_out, new_out, slot_out,
    og, mem, cnt, ids, pick, emb, x32, sqp, cen, g32, sb, recv, xc, cs, rc, idbuf, lbuf, rid, rank, sel, info, ssel, hot, lhs,
    tmax, bloc, rbest, acc, ssq, rssq,
    lsem, cl_s, cl_r, ce_s, ce_r, id_s, id_r, sq_s, sq_r, be_s, be_r,
):
    rows, feat = emb.shape
    n_dp, n_cent = 16, 8
    me = lax.axis_index("dp")
    jc = lax.axis_index("cent")
    mx, my = me // 4, lax.rem(me, 4)
    chunk = rows // 4
    share = pick.shape[1]
    cshard = cen.shape[0]
    lo_n = acc.shape[1]
    fpart = feat // n_dp

    def peer(i):
        k = lax.rem(i * 7, 16)
        return lax.rem(mx + k // 4, 4) * 4 + lax.rem(my + lax.rem(k, 4), 4)

    def cpeer(k):
        return lax.rem(jc + k, n_cent)

    slabs = x32.reshape(rows + 1, 8, 128)

    def load(i):
        return pltpu.make_async_copy(
            emb_hbm.at[pl.ds(i * chunk, chunk)], emb.at[pl.ds(i * chunk, chunk)], lsem.at[i]
        )

    cent_load = pltpu.make_async_copy(cent_hbm, cen, lsem.at[8])
    tables = [
        pltpu.make_async_copy(a, b, lsem.at[9 + i])
        for i, (a, b) in enumerate(((og_hbm, og), (mem_hbm, mem), (cnt_hbm, cnt), (ids_hbm, ids)))
    ]
    for c in tables:
        c.start()
    for i in range(4):
        load(i).start()

    barrier = pltpu.get_barrier_semaphore()
    for k in range(1, n_dp):
        pl.semaphore_signal(barrier, inc=1, device_id={"dp": peer(k)}, device_id_type=MESH)
    for k in range(1, n_cent):
        pl.semaphore_signal(barrier, inc=1, device_id={"cent": cpeer(k)}, device_id_type=MESH)

    x32[rows * 8:, :] = jnp.full((8, 128), jnp.nan, F32)

    def widen_chunk(i, _):
        load(i).wait()

        def widen(n, _):
            r = pl.multiple_of(i * chunk + n * 16, 16)
            square = jnp.zeros((16, 128), F32)
            for c in range(8):
                v = emb[pl.ds(r, 16), c * 128:(c + 1) * 128].astype(F32)
                x32[pl.ds(r * 8 + c, 16, stride=8), :] = v
                square = square + v * v
            sqp[pl.ds(r, 16), :] = square
            return 0

        lax.fori_loop(0, chunk // 16, widen, 0, unroll=4)
        return 0

    lax.fori_loop(0, 4, widen_chunk, 0)
    cent_load.start()
    for c in tables:
        c.wait()
    pl.semaphore_wait(barrier, n_dp + n_cent - 2)

    def gather(t, p, dst):
        g = og[jc, t, p]
        live = cnt[g]
        for q in range(16):
            row = jnp.where(q < live, mem[q, g], rows)
            g32[q * 8:(q + 1) * 8, :] = slabs[row]
        for c in range(8):
            dst[:, c * 128:(c + 1) * 128] = g32[pl.ds(c, 16, stride=8), :].astype(BF16)

    def cl_copy(t, p, s):
        return pltpu.make_async_remote_copy(
            src_ref=sb.at[t, p], dst_ref=recv.at[t, s],
            send_sem=cl_s.at[t, p], recv_sem=cl_r.at[t, s],
            device_id={"dp": p}, device_id_type=MESH,
        )

    def send_round(t):
        def step(k, _):
            p = peer(k)
            gather(t, p, sb.at[t, p])

            @pl.when(k > 0)
            def _():
                cl_copy(t, p, me).start()

            return 0

        lax.fori_loop(0, n_dp, step, 0, unroll=2)
        recv[t, me] = sb[t, me]

    send_round(0)

    idv = ids[...]
    inside = (idv // cshard) == jc
    insf = inside.astype(F32).astype(BF16)
    lane_a = lax.broadcasted_iota(jnp.int32, (128, 128), 0)
    lane_b = lax.broadcasted_iota(jnp.int32, (128, 128), 1)
    upper = (lane_a <= lane_b).astype(F32).astype(BF16)
    run = dot(insf, upper, NN)
    total = dot(insf, jnp.ones((128, 128), BF16), NN).astype(BF16)
    row_a = lax.broadcasted_iota(jnp.int32, (32, 32), 0)
    row_b = lax.broadcasted_iota(jnp.int32, (32, 32), 1)
    lower = (row_b < row_a).astype(F32).astype(BF16)
    before = dot(lower, total, NN)
    rank[0] = jnp.where(inside, before + run - 1.0, -1.0)
    local_id = idv - jc * cshard
    rank[1] = jnp.where(inside, (local_id // 256).astype(F32), 0.0)
    rank[2] = jnp.where(inside, lax.rem(local_id, 256).astype(F32), 0.0)
    want = lax.broadcasted_iota(jnp.int32, (256, 128), 0).astype(F32).astype(BF16)
    sub16 = lax.broadcasted_iota(jnp.int32, (16, 128), 0)
    lane16 = lax.broadcasted_iota(jnp.int32, (16, 128), 1)
    one_b, zero_b = jnp.ones((256, 128), BF16), jnp.zeros((256, 128), BF16)
    ssel[...] = jnp.zeros_like(ssel)

    def select(n, _):
        for v in range(4):
            q = n * 4 + v
            at = slice(v * 128, (v + 1) * 128)
            r = rank[0, pl.ds(q, 1), :]
            for u in range(share // 256):
                ru = jnp.broadcast_to((r - u * 256.0).astype(BF16), (256, 128))
                sel[u * 256:(u + 1) * 256, at] = jnp.where(want == ru, one_b, zero_b)
            place_hi = jnp.zeros((16, 128), jnp.int32) + (n * 2 + v // 2)
            place_lo = lane16 + (v % 2) * 128
            value = jnp.where(sub16 == 0, place_hi, place_lo).astype(F32)
            value = jnp.where(sub16 == 2, rank[1, pl.ds(q, 1), :], value)
            value = jnp.where(sub16 == 3, rank[2, pl.ds(q, 1), :], value)
            info[:, at] = value.astype(BF16)
        ssel[...] += dot(info[...], sel[...], NT)
        return 0

    lax.fori_loop(0, rows // 512, select, 0)
    lbuf[...] = (ssel[0:1, :] * 256.0 + ssel[1:2, :]).astype(jnp.int32)
    to_smem = pltpu.make_async_copy(lbuf, pick, lsem.at[13])
    to_smem.start()
    idbuf[...] = (ssel[2:3, :] * 256.0 + ssel[3:4, :]).astype(jnp.int32)
    rid[me] = idbuf[...]

    def id_copy(p, s):
        return pltpu.make_async_remote_copy(
            src_ref=idbuf, dst_ref=rid.at[s], send_sem=id_s.at[p], recv_sem=id_r.at[s],
            device_id={"dp": p}, device_id_type=MESH,
        )

    def ce_copy(p, s):
        return pltpu.make_async_remote_copy(
            src_ref=cs.at[p], dst_ref=rc.at[s], send_sem=ce_s.at[p], recv_sem=ce_r.at[s],
            device_id={"dp": p}, device_id_type=MESH,
        )

    to_smem.wait()

    def take(n, _):
        for u in range(32):
            p = n * 32 + u
            xc[pl.ds(pl.multiple_of(p * 8, 8), 8), :] = slabs[jnp.clip(pick[0, p], 0, rows - 1)]
        return 0

    lax.fori_loop(0, share // 32, take, 0)
    part = jnp.zeros((share, 128), F32)
    for c in range(8):
        v = xc[pl.ds(c, share, stride=8), :]
        part = part + v * v
    scale = 1.0 / jnp.sqrt(jnp.sum(part, axis=1, keepdims=True) + EPS)
    for c in range(8):
        v = (xc[pl.ds(c, share, stride=8), :] * scale).astype(BF16).T
        cs[2 * c] = v[:fpart]
        cs[2 * c + 1] = v[fpart:]
    rc[me] = cs[me]

    def send_cent(k, _):
        p = peer(k)
        id_copy(p, me).start()
        ce_copy(p, me).start()
        return 0

    lax.fori_loop(1, n_dp, send_cent, 0)

    def later_round(t, _):
        send_round(t)
        return 0

    lax.fori_loop(1, 4, later_round, 0)

    cent_load.wait()

    def unit_cent(n, _):
        r = pl.multiple_of(n * 128, 128)
        v = cen[pl.ds(r, 128), :].astype(F32)
        w = v * (1.0 / jnp.sqrt(jnp.sum(v * v, axis=1, keepdims=True) + EPS))
        cen[pl.ds(r, 128), :] = w.astype(BF16)
        return 0

    lax.fori_loop(0, cshard // 128, unit_cent, 0)

    def sq_copy(p, s):
        return pltpu.make_async_remote_copy(
            src_ref=ssq, dst_ref=rssq.at[s], send_sem=sq_s.at[p], recv_sem=sq_r.at[s],
            device_id={"dp": p}, device_id_type=MESH,
        )

    n_hi = cshard // lo_n
    want_lo = lax.broadcasted_iota(jnp.int32, (lo_n, share), 0).astype(F32).astype(BF16)
    one_s, zero_s = jnp.ones((lo_n, share), BF16), jnp.zeros((lo_n, share), BF16)
    zero_f = jnp.zeros((fpart, share), BF16)

    def place(s, u):
        ident = rid[s]
        low = (ident & (lo_n - 1)).astype(F32).astype(BF16)
        high = (ident // lo_n).astype(F32).astype(BF16)
        at = slice(u * share, (u + 1) * share)
        hot[:, at] = jnp.where(want_lo == jnp.broadcast_to(low, (lo_n, share)), one_s, zero_s)
        x = rc[s]
        hb = jnp.broadcast_to(high, (fpart, share))
        for h in range(n_hi):
            lhs[h * fpart:(h + 1) * fpart, at] = jnp.where(hb == float(h), x, zero_f)

    def arrived(k, _):
        s = peer(k)
        id_copy(s, s).wait_recv()
        ce_copy(s, s).wait_recv()
        return 0

    def add_group(g, _):
        for u in range(4):
            place(peer(g * 4 + u), u)
        acc[...] += dot(lhs[...], hot[...], NT)
        return 0

    def sum_rows():
        lax.fori_loop(1, n_dp, arrived, 0)
        acc[...] = jnp.zeros_like(acc)
        lax.fori_loop(0, 4, add_group, 0)
        for h in range(n_hi):
            a = acc[h * fpart:(h + 1) * fpart, :]
            ssq[h:h + 1, :] = jnp.sum(a * a, axis=0, keepdims=True)
        rssq[me] = ssq[...]

        def send_sq(k, _):
            sq_copy(peer(k), me).start()
            return 0

        lax.fori_loop(1, n_dp, send_sq, 0)

    blk = tmax.shape[0]
    wide = 2048

    def score(b, _):
        pl.when(b == rows // blk - 1)(sum_rows)
        r = pl.multiple_of(b * blk, blk)

        def tile(n, _):
            k0 = pl.multiple_of(n * wide, wide)
            s = dot(emb[pl.ds(r, blk), :], cen[pl.ds(k0, wide), :], NT)
            m = s[:, 0:128]
            for c in range(1, wide // 128):
                m = jnp.maximum(m, s[:, c * 128:(c + 1) * 128])
            tmax[...] = jnp.where(n == 0, m, jnp.maximum(tmax[...], m))
            return 0

        lax.fori_loop(0, cshard // wide, tile, 0)
        top = jnp.max(tmax[...].T, axis=0, keepdims=True)
        nrm = jnp.sqrt(jnp.sum(sqp[pl.ds(r, blk), :].T, axis=0, keepdims=True) + EPS)
        top = top / nrm
        for c in range(blk // 128):
            bloc[pl.ds(b * (blk // 128) + c, 1), :] = top[:, c * 128:(c + 1) * 128]
        return 0

    lax.fori_loop(0, rows // blk, score, 0)

    def be_copy(p, s):
        return pltpu.make_async_remote_copy(
            src_ref=bloc, dst_ref=rbest.at[s], send_sem=be_s.at[p], recv_sem=be_r.at[s],
            device_id={"cent": p}, device_id_type=MESH,
        )

    for k in range(1, n_cent):
        be_copy(cpeer(k), jc).start()

    pa = lax.broadcasted_iota(jnp.int32, (256, 256), 0)
    pb = lax.broadcasted_iota(jnp.int32, (256, 256), 1)
    diag = pa == pb

    def block(t, _):
        def arrive(k, _):
            s = peer(k)
            cl_copy(t, s, s).wait_recv()
            return 0

        lax.fori_loop(1, n_dp, arrive, 0)
        x = recv[t].reshape(256, feat)
        gm = dot(x, x, NT)
        dg = jnp.where(diag, gm, 0.0)
        icol = 1.0 / jnp.sqrt(jnp.sum(dg, axis=1, keepdims=True) + EPS)
        irow = 1.0 / jnp.sqrt(jnp.sum(dg, axis=0, keepdims=True) + EPS)
        v = gm * icol
        ok = (v == v) & jnp.logical_not(diag)
        m = jnp.max(jnp.where(ok, v, -jnp.inf), axis=0, keepdims=True)
        slot_out[pl.ds(t, 1), :] = jnp.where(m > -jnp.inf, m * irow, -1.0)
        return 0

    lax.fori_loop(0, 4, block, 0, unroll=True)

    def got_sq(k, _):
        s = peer(k)
        sq_copy(s, s).wait_recv()
        return 0

    lax.fori_loop(1, n_dp, got_sq, 0)
    full = rssq[0]
    for s in range(1, n_dp):
        full = full + rssq[s]
    inv = 1.0 / jnp.maximum(jnp.sqrt(full), 1.0)
    for h in range(n_hi):
        new_out[:, h * lo_n:(h + 1) * lo_n] = (
            acc[h * fpart:(h + 1) * fpart, :] * inv[h:h + 1, :]
        )

    for k in range(1, n_cent):
        s = cpeer(k)
        be_copy(s, s).wait_recv()
    rbest[jc] = bloc[...]
    top = rbest[0]
    for s in range(1, n_cent):
        top = jnp.maximum(top, rbest[s])
    best_out[...] = top


    def sent(k, _):
        p = peer(k)
        for t in range(4):
            cl_copy(t, p, me).wait_send()
        id_copy(p, me).wait_send()
        ce_copy(p, me).wait_send()
        sq_copy(p, me).wait_send()
        return 0

    lax.fori_loop(1, n_dp, sent, 0)
    for k in range(1, n_cent):
        be_copy(cpeer(k), jc).wait_send()


def hand_over(best, new, slot, best_out, new_out, slot_out):
    best_out[...] = best[...]
    new_out[...] = new[...]
    slot_out[...] = slot[...]


def shards(embeddings, centroids, kmeans_id, members, counts, owner_groups):
    rows, feat = embeddings.shape
    cshard = centroids.shape[0]
    vm = pl.BlockSpec(memory_space=pltpu.VMEM)
    hbm = pl.BlockSpec(memory_space=pltpu.MemorySpace.HBM)
    dma = pltpu.SemaphoreType.DMA
    tables = (
        owner_groups.transpose(1, 2, 0), members[:, 0, :].T,
        counts.reshape(-1), kmeans_id.reshape(32, 128),
    )
    best, new, slot = pl.pallas_call(
        body,
        out_shape=(
            jax.ShapeDtypeStruct((rows // 128, 128), F32),
            jax.ShapeDtypeStruct((feat // 16, cshard), F32),
            jax.ShapeDtypeStruct((4, 256), F32),
        ),
        in_specs=[hbm] * 6,
        out_specs=(vm, vm, vm),
        scratch_shapes=[
            pltpu.SMEM((8, 4, 16), jnp.int32),
            pltpu.SMEM((16, 512), jnp.int32),
            pltpu.SMEM((512,), jnp.int32),
            pltpu.VMEM((rows // 128, 128), jnp.int32),
            pltpu.SMEM((1, 512), jnp.int32),
            pltpu.VMEM((rows, feat), BF16),
            pltpu.VMEM((rows * 8 + 8, 128), F32),
            pltpu.VMEM((rows, 128), F32),
            pltpu.VMEM((cshard, feat), BF16),
            pltpu.VMEM((128, 128), F32),
            pltpu.VMEM((4, 16, 16, feat), BF16),
            pltpu.VMEM((4, 16, 16, feat), BF16),
            pltpu.VMEM((512 * 8, 128), F32),
            pltpu.VMEM((16, feat // 16, 512), BF16),
            pltpu.VMEM((16, feat // 16, 512), BF16),
            pltpu.VMEM((1, 512), jnp.int32),
            pltpu.VMEM((1, 512), jnp.int32),
            pltpu.VMEM((16, 1, 512), jnp.int32),
            pltpu.VMEM((3, 32, 128), F32),
            pltpu.VMEM((512, 512), BF16),
            pltpu.VMEM((16, 512), BF16),
            pltpu.VMEM((16, 512), F32),
            pltpu.VMEM((256, 2048), BF16),
            pltpu.VMEM((512, 2048), BF16),
            pltpu.VMEM((1024, 128), F32),
            pltpu.VMEM((rows // 128, 128), F32),
            pltpu.VMEM((8, rows // 128, 128), F32),
            pltpu.VMEM((512, 256), F32),
            pltpu.VMEM((8, 256), F32),
            pltpu.VMEM((16, 8, 256), F32),
            dma((14,)),
            dma((4, 16)), dma((4, 16)),
            dma((16,)), dma((16,)),
            dma((16,)), dma((16,)),
            dma((16,)), dma((16,)),
            dma((8,)), dma((8,)),
        ],
        compiler_params=pltpu.CompilerParams(
            collective_id=0, has_side_effects=True, vmem_limit_bytes=50 << 20
        ),
        name="window",
    )(
        *(pltpu.with_memory_space_constraint(v, pltpu.MemorySpace.HBM) for v in tables),
        embeddings,
        centroids,
    )
    best, new, slot = pl.pallas_call(
        hand_over,
        out_shape=tuple(jax.ShapeDtypeStruct(v.shape, v.dtype) for v in (best, new, slot)),
        in_specs=[vm, vm, vm],
        out_specs=(vm, vm, vm),
        compiler_params=pltpu.CompilerParams(vmem_limit_bytes=4 << 20),
        name="hand_over",
    )(best, new, slot)
    return best.reshape(rows), new, slot.reshape(1, 1, 4, 256)


def solution(mesh):
    placed = (P("dp", None), P("cent", None), P("dp"), P(None, "dp", None), P(None, "dp"), P())
    return jax.shard_map(
        shards,
        mesh=mesh,
        in_specs=placed,
        out_specs=(P("dp"), P("dp", "cent"), P("dp", "cent", None, None)),
        check_vma=False,
    )
```
